32 devices in a mesh: grp: 8 (over z, y), mem: 4 (over x, core).
Axes of the slice: x: 2, y: 2, z: 4, core: 2. Of those that a mesh axis runs over, the one named last changes fastest.
Arguments:
- tiles: bfloat16 [192, 11, 256, 256], P(('grp', 'mem')), as said below
- mask: int32 [192, 11], P(('grp', 'mem')), may hold values from 0 to 1, as said below
- branch: int32 [192], P(('grp', 'mem')), may hold values from 0 to 1
Outputs:
- new_tiles: float32 [192, 11, 256, 256], P(('grp', 'mem'))
- traces: float32 [2], replicated
The draws below stay inside these ranges and needn't reach their ends.
Inputs may be any that keep to these rules, and one draw needn't show every extreme that they name: X is symmetric: for |d| <= 5, wherever rows i and i + d both lie in the matrix, tiles[i + d, 5 - d] is exactly the transpose of tiles[i, 5 + d]. mask is symmetric in the same way (mask[i + d, 5 - d] == mask[i, 5 + d]); the diagonal slot mask[i, 5] is always 1; slots whose column i - 5 + s lies outside the matrix are 0.
All inputs are finite; a program needn't handle non-finite values.
Results may differ from the reference program's by a relative error of at most 0.0003.
Values may be sent and summed in bfloat16 or wider, within the bound.
A program may use at most 256 MiB of HBM per device.

```python
import math
import jax
import jax.numpy as jnp
from jax import lax

TILE = 256
BAND = 5
ROWS_DEV = 6
SLOTS = 11
NTILES = 192
ORDER = 49152


def draw_tiles(key, part):
    subkeys = jax.random.split(key, 4)
    spread = 0.8 / math.sqrt(TILE)
    upper_draw = jax.random.normal(subkeys[0], (NTILES, BAND, TILE, TILE), jnp.float32)
    centre_draw = jax.random.normal(subkeys[1], (NTILES, TILE, TILE), jnp.float32)
    position = jnp.arange(ORDER, dtype=jnp.float32) / ORDER
    row_scale = (0.8 + 0.6 * position).reshape(NTILES, TILE)
    diagonal = jax.random.uniform(subkeys[3], (NTILES, TILE), jnp.float32, 0.2, 1.0)
    mirrored = (centre_draw + jnp.swapaxes(centre_draw, 1, 2)) * (0.5 * spread)
    mirrored = mirrored + jnp.eye(TILE, dtype=jnp.float32)[None] * diagonal[:, :, None]
    middle = mirrored * (row_scale[:, :, None] * row_scale[:, None, :])
    above_tiles = []
    for offset in range(1, BAND + 1):
        partner = jnp.roll(row_scale, -offset, axis=0)
        above_tiles.append(upper_draw[:, offset - 1] * spread * (row_scale[:, :, None] * partner[:, None, :]))
    below_tiles = [jnp.swapaxes(jnp.roll(above_tiles[offset - 1], offset, axis=0), 1, 2) for offset in range(BAND, 0, -1)]
    return jnp.stack(below_tiles + [middle] + above_tiles, axis=1).astype(jnp.bfloat16)


def draw_mask(key, part):
    subkeys = jax.random.split(key, 2)
    level_index = jax.random.randint(subkeys[0], (NTILES // ROWS_DEV,), 0, 4)
    level_table = jnp.array([20, 35, 50, 100], dtype=jnp.int32)
    row_levels = jnp.repeat(jnp.take(level_table, level_index), ROWS_DEV)
    coin_draw = jax.random.randint(subkeys[1], (NTILES, BAND), 0, 100)
    upper_mask = (coin_draw < row_levels[:, None]).astype(jnp.int32)
    indices = jnp.arange(NTILES, dtype=jnp.int32)
    columns = []
    for slot_index in range(SLOTS):
        offset = slot_index - BAND
        if offset == 0:
            columns.append(jnp.ones((NTILES,), jnp.int32))
        elif offset > 0:
            columns.append(upper_mask[:, offset - 1] * (indices + offset < NTILES).astype(jnp.int32))
        else:
            distance = -offset
            columns.append(jnp.roll(upper_mask[:, distance - 1], distance) * (indices - distance >= 0).astype(jnp.int32))
    return jnp.stack(columns, axis=1)


def place_ends(values, key, least, largest):
    shape = values.shape
    place = [jax.random.randint(jax.random.fold_in(key, axis), (), 0, shape[axis]) for axis in range(len(shape))]
    values = values.at[tuple(place)].set(least)
    longest = shape.index(max(shape))
    place[longest] = (place[longest] + 1) % shape[longest]
    return values.at[tuple(place)].set(largest)


def setup_inputs(seed: int = 0) -> dict:
    keys = jax.random.split(jax.random.key(seed), 4)
    tiles = draw_tiles(jax.random.fold_in(keys[3], 71), 0)
    mask = draw_mask(jax.random.fold_in(keys[3], 71), 0)
    branch = place_ends(jax.random.randint(keys[2], (NTILES,), 0, 2), jax.random.fold_in(keys[2], 1), 0, 1).astype(jnp.int32)
    return {"tiles": tiles, "mask": mask, "branch": branch}


def band_square(extended, row_count, half_band, slot_count):
    pieces = []
    for column in range(slot_count):
        first_slot = max(0, column - half_band)
        last_slot = min(slot_count - 1, column + half_band)
        left_tiles = extended[half_band:half_band + row_count, first_slot:last_slot + 1].astype(jnp.float32)
        right_tiles = jnp.stack([extended[through:through + row_count, column - through + half_band] for through in range(first_slot, last_slot + 1)], axis=1).astype(jnp.float32)
        pieces.append(jnp.einsum("rpab,rpbc->rac", left_tiles, right_tiles))
    return jnp.stack(pieces, axis=1)


def reference(tiles, mask, branch):
    occupied = mask[:, :, None, None]
    masked = tiles * occupied.astype(tiles.dtype)
    padded = jnp.pad(masked, ((BAND, BAND), (0, 0), (0, 0), (0, 0)))

    def square_block(first_row):
        window = lax.dynamic_slice_in_dim(padded, first_row, ROWS_DEV + 2 * BAND, 0)
        square = band_square(window, ROWS_DEV, BAND, SLOTS)
        own_rows = lax.dynamic_slice_in_dim(masked, first_row, ROWS_DEV, 0).astype(jnp.float32)
        keeper = lax.dynamic_slice_in_dim(occupied, first_row, ROWS_DEV, 0).astype(jnp.float32)
        selector = lax.dynamic_slice_in_dim(branch, first_row, ROWS_DEV, 0)[:, None, None, None]
        updated = jnp.where(selector == 0, square, 2.0 * own_rows - square) * keeper
        trace_part = jnp.sum(jnp.diagonal(updated[:, BAND], axis1=1, axis2=2))
        purity_part = jnp.sum(updated * updated)
        return updated, trace_part, purity_part

    starts = jnp.arange(NTILES // ROWS_DEV, dtype=jnp.int32) * ROWS_DEV
    updated, trace_parts, purity_parts = lax.map(square_block, starts)
    new_tiles = updated.reshape(NTILES, SLOTS, TILE, TILE)
    traces = jnp.stack([jnp.sum(trace_parts), jnp.sum(purity_parts)]) / ORDER
    return new_tiles, traces
```

```python
import functools

import jax
import jax.numpy as jnp
from jax import lax
from jax.experimental import pallas as pl
from jax.experimental.pallas import tpu as pltpu
from jax.sharding import PartitionSpec as P


ANY = pl.BlockSpec(memory_space=pl.ANY)
SMEM = pl.BlockSpec(memory_space=pltpu.SMEM)
VMEM_ALL = pl.BlockSpec(memory_space=pltpu.VMEM)
BIG = 60 * 2**20


def nn(left, right):
    return jnp.dot(left, right, preferred_element_type=jnp.float32)


def nt(left, right):
    return lax.dot_general(
        left, right, (((1,), (1,)), ((), ())), preferred_element_type=jnp.float32
    )


def finish(square, own, mask, branch):
    value = jnp.where(branch == 0, square, 2.0 * own.astype(jnp.float32) - square)
    return jnp.where(mask != 0, value, 0.0)


def fold(value):
    return jnp.sum(value.reshape(value.shape[0] // 8, 8, value.shape[1]), axis=0)


def corner_lists(half):
    upper_far = [(c, 0) for c in range(half)]
    upper_near = [(c, b) for c in range(1, half) for b in range(1, c + 1)]
    lower_far = [(half - 1, b) for b in range(half)]
    lower_near = [(c, b) for c in range(half - 1) for b in range(c + 1)]
    return upper_near, upper_far, lower_near, lower_far


def pack(tiles, mask, upper_list, lower_list):
    rows, slots, side, _ = tiles.shape
    half = (slots - 1) // 2
    sources = [(rows - half + c, b - c + half) for c, b in upper_list]
    sources += [(c, b - c + half) for c, b in lower_list]
    count = len(upper_list)

    def kernel(tiles_ref, mask_ref, down_ref, up_ref, held, in_sem, out_sem):
        for index, (row, slot) in enumerate(sources):
            pltpu.make_async_copy(tiles_ref.at[row, slot], held.at[index], in_sem.at[index]).start()
        outs = []
        for index, (row, slot) in enumerate(sources):
            pltpu.make_async_copy(tiles_ref.at[row, slot], held.at[index], in_sem.at[index]).wait()

            @pl.when(mask_ref[row, slot] == 0)
            def _():
                held[index] = jnp.zeros((side, side), tiles.dtype)

            target = down_ref.at[index] if index < count else up_ref.at[index - count]
            out = pltpu.make_async_copy(held.at[index], target, out_sem.at[index])
            out.start()
            outs.append(out)
        for out in outs:
            out.wait()

    total = len(sources)
    return pl.pallas_call(
        kernel,
        out_shape=(
            jax.ShapeDtypeStruct((count, side, side), tiles.dtype),
            jax.ShapeDtypeStruct((total - count, side, side), tiles.dtype),
        ),
        in_specs=[ANY, SMEM],
        out_specs=(ANY, ANY),
        scratch_shapes=[
            pltpu.VMEM((total, side, side), tiles.dtype),
            pltpu.SemaphoreType.DMA((total,)),
            pltpu.SemaphoreType.DMA((total,)),
        ],
        compiler_params=pltpu.CompilerParams(vmem_limit_bytes=BIG),
        cost_estimate=pl.CostEstimate(
            flops=0, transcendentals=0, bytes_accessed=4 * total * side * side
        ),
        name="pack",
    )(tiles, mask)


def local_part(tiles, mask, branch):
    rows, slots, side, _ = tiles.shape
    half = (slots - 1) // 2

    def kernel(
        tiles_ref, mask_ref, branch_ref, out_ref, stats_ref,
        own, left, right, staged, in_sem, out_sem,
    ):
        def cols(start, count):
            return pl.ds(start * side, count * side)

        copies = []
        for row in range(rows):
            for slot in range(slots):
                copies.append(
                    pltpu.make_async_copy(
                        tiles_ref.at[row, slot], own.at[row, :, cols(slot, 1)], in_sem.at[row]
                    )
                )
        for copy in copies:
            copy.start()
        stats_ref[...] = jnp.zeros_like(stats_ref)
        for copy in copies:
            copy.wait()
        for row in range(rows):
            for slot in range(slots):

                @pl.when(mask_ref[row, slot] == 0)
                def _():
                    own[row, :, cols(slot, 1)] = jnp.zeros((side, side), own.dtype)

        for k in range(half):
            for b in range(k, half):
                left[cols(k, 1), cols(b, 1)] = own[k, :, cols(b - k, 1)]
        for k in range(half):
            row = rows - half + k
            for b in range(k + 1):
                right[cols(k, 1), cols(b, 1)] = own[row, :, cols(rows + b - row + half, 1)]

        def send(row, slot):
            pltpu.make_async_copy(staged.at[row, slot], out_ref.at[row, slot], out_sem).start()

        def settle(row, slot, square):
            start = pl.multiple_of(slot * side, side)
            value = finish(
                square, own[row, :, pl.ds(start, side)], mask_ref[row, slot], branch_ref[row]
            )
            staged[row, slot] = value
            stats_ref[0:8] += fold(value * value)
            send(row, slot)
            return value

        @pl.loop(0, rows)
        def _(row):
            for d in range(half + 1):

                @pl.when(row + d < rows)
                def _():
                    square = nt(
                        own[row, :, cols(d, slots - d)], own[row + d, :, cols(0, slots - d)]
                    )
                    value = settle(row, half + d, square)
                    if d == 0:
                        on = lax.broadcasted_iota(jnp.int32, value.shape, 0) == (
                            lax.broadcasted_iota(jnp.int32, value.shape, 1)
                        )
                        stats_ref[8:16] += fold(jnp.where(on, value, 0.0))
                    else:
                        settle(row + d, half - d, square.T)

            for b in range(half):
                @pl.when(row <= b)
                def _():
                    start = pl.multiple_of((half - row) * side, side)
                    part = nn(
                        own[row, :, pl.ds(start, (b + 1) * side)],
                        left[cols(0, b + 1), cols(b, 1)],
                    )
                    staged[row, b - row] = part
                    send(row, b - row)

                @pl.when(row >= rows - half + b)
                def _():
                    first = rows - half + b
                    start = pl.multiple_of((first - row + half) * side, side)
                    part = nn(
                        own[row, :, pl.ds(start, (half - b) * side)],
                        right[cols(b, half - b), cols(b, 1)],
                    )
                    slot = rows + b - row + half
                    staged[row, slot] = part
                    send(row, slot)

        pltpu.make_async_copy(staged, out_ref, out_sem).wait()

    matmuls = 300
    return pl.pallas_call(
        kernel,
        out_shape=(
            jax.ShapeDtypeStruct(tiles.shape, jnp.float32),
            jax.ShapeDtypeStruct((16, side), jnp.float32),
        ),
        in_specs=[ANY, SMEM, SMEM],
        out_specs=(ANY, VMEM_ALL),
        scratch_shapes=[
            pltpu.VMEM((rows, side, slots * side), tiles.dtype),
            pltpu.VMEM((half * side, half * side), tiles.dtype),
            pltpu.VMEM((half * side, half * side), tiles.dtype),
            pltpu.VMEM((rows, slots, side, side), jnp.float32),
            pltpu.SemaphoreType.DMA((rows,)),
            pltpu.SemaphoreType.DMA,
        ],
        compiler_params=pltpu.CompilerParams(vmem_limit_bytes=BIG),
        cost_estimate=pl.CostEstimate(
            flops=2 * matmuls * side**3, transcendentals=0, bytes_accessed=6 * tiles.size
        ),
        name="local_part",
    )(tiles, mask, branch)


def halo_part(tiles, mask, branch, partial, above, below, far):
    rows, slots, side, _ = tiles.shape
    half = (slots - 1) // 2
    upper_near, upper_far, lower_near, lower_far = corner_lists(half)
    upper_list, lower_list = (upper_far, lower_far) if far else (upper_near, lower_near)

    jobs = []
    if far:
        jobs += [(0, 0, b, b, True) for b in range(half)]
        jobs += [(rows - 1, 1, b, half + 1 + b, True) for b in range(half)]
    else:
        for a in range(half):
            jobs += [(a, 0, b, b - a, a > 0) for b in range(max(a, 1), half)]
        for a in range(half):
            row = rows - 1 - a
            jobs += [
                (row, 1, b, rows + b - row + half, a > 0)
                for b in range(half - max(a, 1))
            ]
    needed = []
    for a in range(1 if far else half):
        needed += [(a, slot) for slot in range(half - a)]
        needed += [(rows - 1 - a, slot) for slot in range(half + 1 + a, slots)]

    def kernel(
        tiles_ref, mask_ref, branch_ref, partial_ref, above_ref, below_ref,
        out_ref, stats_ref, own, corners, staged, own_sem, corner_sem, in_sem, out_sem,
    ):
        def cols(start, count):
            return pl.ds(start * side, count * side)

        loads = []
        for source, pairs, which in ((above_ref, upper_list, 0), (below_ref, lower_list, 1)):
            for index, (c, b) in enumerate(pairs):
                loads.append(
                    pltpu.make_async_copy(
                        source.at[index],
                        corners.at[which, cols(c, 1), cols(b, 1)],
                        corner_sem,
                    )
                )
        for row, slot in needed:
            loads.append(
                pltpu.make_async_copy(
                    tiles_ref.at[row, slot], own.at[row, :, cols(slot, 1)], own_sem
                )
            )
        parts = [
            pltpu.make_async_copy(partial_ref.at[row, slot], staged.at[index], in_sem.at[index])
            for index, (row, _, _, slot, _) in enumerate(jobs)
        ]
        for copy in loads + parts:
            copy.start()
        stats_ref[...] = jnp.zeros_like(stats_ref)
        for copy in loads:
            copy.wait()
        for row, slot in needed:

            @pl.when(mask_ref[row, slot] == 0)
            def _():
                own[row, :, cols(slot, 1)] = jnp.zeros((side, side), own.dtype)

        outs = []
        total = jnp.zeros((8, side), jnp.float32)
        for index, (row, which, b, slot, final) in enumerate(jobs):
            base = -row if which == 0 else rows - row + half
            held = corners.at[which]

            def straight(low, high):
                return nn(own[row, :, cols(base + low, high - low)], held[cols(low, high - low), cols(b, 1)])

            def turned(low, high):
                return nt(own[row, :, cols(base + low, high - low)], held[cols(b, 1), cols(low, high - low)])

            if far and which == 0:
                product = straight(0, half) if b == 0 else turned(0, 1)
            elif far:
                product = turned(0, half) if b == half - 1 else straight(half - 1, half)
            else:
                if which == 0:
                    low, high = max(row, 1), half
                else:
                    low, high = 0, half - max(rows - 1 - row, 1)
                product = straight(b, high)
                if b > low:
                    product = product + turned(low, b)
            parts[index].wait()
            square = staged[index] + product
            if final:
                value = finish(
                    square, own[row, :, cols(slot, 1)], mask_ref[row, slot], branch_ref[row]
                )
                total = total + fold(value * value)
            else:
                value = square
            staged[index] = value
            out = pltpu.make_async_copy(staged.at[index], out_ref.at[row, slot], out_sem.at[index])
            out.start()
            outs.append(out)
        stats_ref[0:8] = total
        for out in outs:
            out.wait()

    count = len(jobs)
    return pl.pallas_call(
        kernel,
        out_shape=(
            jax.ShapeDtypeStruct(tiles.shape, jnp.float32),
            jax.ShapeDtypeStruct((16, side), jnp.float32),
        ),
        in_specs=[ANY, SMEM, SMEM, ANY, ANY, ANY],
        out_specs=(ANY, VMEM_ALL),
        scratch_shapes=[
            pltpu.VMEM((rows, side, slots * side), tiles.dtype),
            pltpu.VMEM((2, half * side, half * side), tiles.dtype),
            pltpu.VMEM((count, side, side), jnp.float32),
            pltpu.SemaphoreType.DMA,
            pltpu.SemaphoreType.DMA,
            pltpu.SemaphoreType.DMA((count,)),
            pltpu.SemaphoreType.DMA((count,)),
        ],
        input_output_aliases={3: 0},
        compiler_params=pltpu.CompilerParams(vmem_limit_bytes=BIG),
        cost_estimate=pl.CostEstimate(
            flops=2 * (18 if far else 92) * side**3,
            transcendentals=0,
            bytes_accessed=12 * count * side * side,
        ),
        name="halo_far" if far else "halo_near",
    )(tiles, mask, branch, partial, above, below)


def total_stats(stats, order, groups, members):
    def kernel(*refs):
        stat_refs = refs[: len(stats)]
        out_ref, mine, group, first, second, send_sem, first_sem, second_sem = refs[len(stats) :]
        g, m = lax.axis_index("grp"), lax.axis_index("mem")
        barrier = pltpu.get_barrier_semaphore()

        def greet_member(step, carry):
            other = lax.rem(m + step, members)
            pl.semaphore_signal(barrier, 1, device_id=(g, other), device_id_type=pl.DeviceIdType.MESH)
            return carry

        def greet_group(step, carry):
            other = lax.rem(g + step, groups)
            pl.semaphore_signal(barrier, 1, device_id=(other, m), device_id_type=pl.DeviceIdType.MESH)
            return carry

        lax.fori_loop(1, members, greet_member, 0)
        lax.fori_loop(1, groups, greet_group, 0)
        summed = stat_refs[0][...]
        for ref in stat_refs[1:]:
            summed = summed + ref[...]
        purity = jnp.sum(summed[0:8])
        trace = jnp.sum(summed[8:16])
        lane = lax.broadcasted_iota(jnp.int32, (8, 128), 1)
        mine[...] = jnp.where(lane == 0, trace, purity)
        pl.semaphore_wait(barrier, members + groups - 2)

        def exchange(source, slots, sems, me, count, device, offset):
            def copy(step):
                other = lax.rem(me + step, count)
                return pltpu.make_async_remote_copy(
                    source, slots.at[me], send_sem.at[offset + step], sems.at[me],
                    device_id=device(other), device_id_type=pl.DeviceIdType.MESH,
                )

            def arrival(step):
                other = lax.rem(me + step, count)
                return pltpu.make_async_remote_copy(
                    source, slots.at[other], send_sem.at[offset + step], sems.at[other],
                    device_id=device(other), device_id_type=pl.DeviceIdType.MESH,
                )

            def begin(step, carry):
                copy(step).start()
                return carry

            def end(step, carry):
                arrival(step).wait_recv()
                return carry

            def leave(step, carry):
                copy(step).wait_send()
                return carry

            lax.fori_loop(1, count, begin, 0)
            slots[me] = source[...]
            lax.fori_loop(1, count, end, 0)
            result = slots[0]
            for index in range(1, count):
                result = result + slots[index]
            return result, functools.partial(lax.fori_loop, 1, count, leave, 0)

        group_sum, leave_first = exchange(
            mine, first, first_sem, m, members, lambda other: (g, other), 0
        )
        group[...] = group_sum
        whole, leave_second = exchange(
            group, second, second_sem, g, groups, lambda other: (other, m), members
        )
        out_ref[...] = whole / order
        leave_first()
        leave_second()

    result = pl.pallas_call(
        kernel,
        out_shape=jax.ShapeDtypeStruct((8, 128), jnp.float32),
        in_specs=[VMEM_ALL] * len(stats),
        out_specs=VMEM_ALL,
        scratch_shapes=[
            pltpu.VMEM((8, 128), jnp.float32),
            pltpu.VMEM((8, 128), jnp.float32),
            pltpu.VMEM((members, 8, 128), jnp.float32),
            pltpu.VMEM((groups, 8, 128), jnp.float32),
            pltpu.SemaphoreType.DMA((members + groups,)),
            pltpu.SemaphoreType.DMA((members,)),
            pltpu.SemaphoreType.DMA((groups,)),
        ],
        compiler_params=pltpu.CompilerParams(collective_id=0, has_side_effects=True),
        name="total_stats",
    )(*stats)
    return result[0, 0:2]


def on_device(tiles, mask, branch, groups, members):
    rows, slots, side, _ = tiles.shape
    half = (slots - 1) // 2
    devices = groups * members
    upper_near, upper_far, lower_near, lower_far = corner_lists(half)
    axes = ("grp", "mem")
    forward = [(index, index + 1) for index in range(devices - 1)]
    backward = [(index + 1, index) for index in range(devices - 1)]

    down_near, up_near = pack(tiles, mask, upper_near, lower_near)
    above_near = lax.ppermute(down_near, axes, forward)
    below_near = lax.ppermute(up_near, axes, backward)
    down_far, up_far = pack(tiles, mask, upper_far, lower_far)
    above_far = lax.ppermute(down_far, axes, forward)
    below_far = lax.ppermute(up_far, axes, backward)

    partial, local_stats = local_part(tiles, mask, branch)
    partial, near_stats = halo_part(
        tiles, mask, branch, partial, above_near, below_near, False
    )
    updated, far_stats = halo_part(tiles, mask, branch, partial, above_far, below_far, True)
    order = float(rows * devices * side)
    traces = total_stats((local_stats, near_stats, far_stats), order, groups, members)
    return updated, traces


def solution(mesh):
    placed = (P(("grp", "mem"), None, None, None), P(("grp", "mem"), None), P(("grp", "mem")))
    return jax.shard_map(
        functools.partial(
            on_device, groups=mesh.shape["grp"], members=mesh.shape["mem"]
        ),
        mesh=mesh,
        in_specs=placed,
        out_specs=(P(("grp", "mem"), None, None, None), P()),
        check_vma=False,
    )
```

```python
import functools

import jax
import jax.numpy as jnp
from jax import lax
from jax.experimental import pallas as pl
from jax.experimental.pallas import tpu as pltpu
from jax.sharding import PartitionSpec as P


ANY = pl.BlockSpec(memory_space=pl.ANY)
SMEM = pl.BlockSpec(memory_space=pltpu.SMEM)
VMEM_ALL = pl.BlockSpec(memory_space=pltpu.VMEM)


def nn(left, right):
    return jnp.dot(left, right, preferred_element_type=jnp.float32)


def nt(left, right):
    return lax.dot_general(
        left, right, (((1,), (1,)), ((), ())), preferred_element_type=jnp.float32
    )


def finish(square, own, mask, branch):
    value = jnp.where(branch == 0, square, 2.0 * own.astype(jnp.float32) - square)
    return jnp.where(mask != 0, value, 0.0)


def fold(value):
    return jnp.sum(value.reshape(value.shape[0] // 8, 8, value.shape[1]), axis=0)


def corner_lists(half):
    upper_near = [(c, b) for b in range(1, half) for c in range(b, half)]
    upper_far = [(c, 0) for c in range(half)]
    lower_near = [(c, b) for b in range(half - 1) for c in range(b, half - 1)]
    lower_far = [(half - 1, b) for b in range(half)]
    return upper_near, upper_far, lower_near, lower_far


def triangle(count):
    return count * (count + 1) // 2


def pack(tiles, mask, lists):
    rows, slots, side, _ = tiles.shape
    half = (slots - 1) // 2
    upper_near, upper_far, lower_near, lower_far = lists
    order = (upper_near, lower_near, upper_far, lower_far)
    sources = []
    for which, pairs in enumerate(order):
        for index, (c, b) in enumerate(pairs):
            row = rows - half + c if which % 2 == 0 else c
            sources.append((which, index, row, b - c + half))

    def kernel(tiles_ref, mask_ref, *refs):
        outs, (held, in_sem, out_sem) = refs[:4], refs[4:]
        loads = [
            pltpu.make_async_copy(tiles_ref.at[row, slot], held.at[place], in_sem.at[place])
            for place, (_, _, row, slot) in enumerate(sources)
        ]
        for load in loads:
            load.start()
        stores = []
        for place, (which, index, row, slot) in enumerate(sources):
            loads[place].wait()

            @pl.when(mask_ref[row, slot] == 0)
            def _():
                held[place] = jnp.zeros((side, side), tiles.dtype)

            store = pltpu.make_async_copy(held.at[place], outs[which].at[index], out_sem.at[place])
            store.start()
            stores.append(store)
        for store in stores:
            store.wait()

    total = len(sources)
    return pl.pallas_call(
        kernel,
        out_shape=tuple(
            jax.ShapeDtypeStruct((len(pairs), side, side), tiles.dtype) for pairs in order
        ),
        in_specs=[pl.BlockSpec(memory_space=pltpu.HBM), SMEM],
        out_specs=(ANY,) * 4,
        scratch_shapes=[
            pltpu.VMEM((total, side, side), tiles.dtype),
            pltpu.SemaphoreType.DMA((total,)),
            pltpu.SemaphoreType.DMA((total,)),
        ],
        compiler_params=pltpu.CompilerParams(vmem_limit_bytes=8 * 2**20),
        cost_estimate=pl.CostEstimate(
            flops=0, transcendentals=0, bytes_accessed=4 * total * side * side
        ),
        name="pack",
    )(pltpu.with_memory_space_constraint(tiles, pltpu.HBM), mask)


def local_part(tiles, mask, branch):
    rows, slots, side, _ = tiles.shape
    half = (slots - 1) // 2
    corner = triangle(half)

    def kernel(
        tiles_ref, mask_ref, branch_ref, out_ref, stats_ref, own, cross,
        left, right, staged, in_sem, out_sem,
    ):
        def cols(start, count):
            return pl.ds(start * side, count * side)

        copies = []
        for row in range(rows):
            for slot in range(slots):
                copies.append(
                    pltpu.make_async_copy(
                        tiles_ref.at[row, slot], own.at[row, :, cols(slot, 1)], in_sem
                    )
                )
        for copy in copies:
            copy.start()
        stats_ref[...] = jnp.zeros_like(stats_ref)
        for copy in copies:
            copy.wait()
        for row in range(rows):
            for slot in range(slots):

                @pl.when(mask_ref[row, slot] == 0)
                def _():
                    own[row, :, cols(slot, 1)] = jnp.zeros((side, side), own.dtype)

        for k in range(half):
            for b in range(k, half):
                left[cols(k, 1), cols(b, 1)] = own[k, :, cols(b - k, 1)]
        for k in range(half):
            row = rows - half + k
            for b in range(k + 1):
                right[cols(k, 1), cols(b, 1)] = own[row, :, cols(rows + b - row + half, 1)]

        def out_copy(row, column):
            return pltpu.make_async_copy(
                staged.at[row, column], out_ref.at[row, column - row + half], out_sem
            )

        def settle(row, column, square):
            slot = column - row + half
            start = pl.multiple_of(slot * side, side)
            value = finish(
                square, own[row, :, pl.ds(start, side)], mask_ref[row, slot], branch_ref[row]
            )
            staged[row, column] = value
            stats_ref[0:8] += fold(value * value)
            out_copy(row, column).start()
            return value

        @pl.loop(0, rows)
        def _(row):
            for d in range(half + 1):

                @pl.when(row + d < rows)
                def _():
                    square = nt(
                        own[row, :, cols(d, slots - d)], own[row + d, :, cols(0, slots - d)]
                    )
                    value = settle(row, row + d, square)
                    if d == 0:
                        on = lax.broadcasted_iota(jnp.int32, value.shape, 0) == (
                            lax.broadcasted_iota(jnp.int32, value.shape, 1)
                        )
                        stats_ref[8:16] += fold(jnp.where(on, value, 0.0))
                    else:
                        settle(row + d, row, square.T)

            for b in range(half):
                @pl.when(row <= b)
                def _():
                    start = pl.multiple_of((half - row) * side, side)
                    cross[triangle(b) + row] = nn(
                        own[row, :, pl.ds(start, (b + 1) * side)],
                        left[cols(0, b + 1), cols(b, 1)],
                    )

                @pl.when(row >= rows - half + b)
                def _():
                    first = rows - half + b
                    start = pl.multiple_of((first - row + half) * side, side)
                    cross[corner + triangle(half - 1 - b) + rows - 1 - row] = nn(
                        own[row, :, pl.ds(start, (half - b) * side)],
                        right[cols(b, half - b), cols(b, 1)],
                    )

        for row in range(rows):
            for column in range(rows):
                if abs(row - column) <= half:
                    out_copy(row, column).wait()

    matmuls = 300
    return pl.pallas_call(
        kernel,
        out_shape=(
            jax.ShapeDtypeStruct(tiles.shape, jnp.float32),
            jax.ShapeDtypeStruct((16, side), jnp.float32),
            pltpu.VMEM((rows, side, slots * side), tiles.dtype),
            pltpu.VMEM((2 * corner, side, side), jnp.float32),
        ),
        in_specs=[ANY, SMEM, SMEM],
        out_specs=(ANY, VMEM_ALL, VMEM_ALL, VMEM_ALL),
        scratch_shapes=[
            pltpu.VMEM((half * side, half * side), tiles.dtype),
            pltpu.VMEM((half * side, half * side), tiles.dtype),
            pltpu.VMEM((rows, rows, side, side), jnp.float32),
            pltpu.SemaphoreType.DMA,
            pltpu.SemaphoreType.DMA,
        ],
        compiler_params=pltpu.CompilerParams(vmem_limit_bytes=22 * 2**20),
        cost_estimate=pl.CostEstimate(
            flops=2 * matmuls * side**3, transcendentals=0, bytes_accessed=6 * tiles.size
        ),
        name="local_part",
    )(tiles, mask, branch)


def halo_part(own, mask, branch, square, partial, above, below, lists, far):
    rows, side, width = own.shape
    slots = width // side
    half = (slots - 1) // 2
    corner = triangle(half)
    upper_near, upper_far, lower_near, lower_far = lists
    places = [
        {pair: index for index, pair in enumerate(pairs)}
        for pairs in ((upper_far, lower_far) if far else (upper_near, lower_near))
    ]

    jobs = []
    if far:
        jobs += [(0, 0, b, b, b, None) for b in range(half)]
        jobs += [(rows - 1, 1, b, half + 1 + b, half + b, None) for b in range(half)]
    else:
        for a in range(half):
            for b in range(a, half):
                jobs.append((a, 0, b, b - a, triangle(b) + a, None if a else b))
            row = rows - 1 - a
            for b in range(half - a):
                place = corner + triangle(half - 1 - b) + a
                jobs.append((row, 1, b, rows + b - row + half, place, None if a else half + b))
    finals = sum(job[5] is None for job in jobs)

    def kernel(own_ref, mask_ref, branch_ref, square_ref, partial_ref, above_ref, below_ref, *refs):
        if far:
            out_ref, stats_ref, staged, out_sem = refs
        else:
            out_ref, stats_ref, edge_ref, staged, out_sem = refs

        def cols(start, count):
            return pl.ds(start * side, count * side)

        outs = []
        stats_ref[...] = jnp.zeros_like(stats_ref)
        for row, which, b, slot, place, edge in jobs:
            held = (above_ref, below_ref)[which]
            where = places[which]
            base = -row if which == 0 else rows - row + half

            def straight(low, high):
                first = where[low, b]
                block = held[first : first + high - low].reshape((high - low) * side, side)
                return nn(own_ref[row, :, cols(base + low, high - low)], block)

            def turned(c):
                return nt(own_ref[row, :, cols(base + c, 1)], held[where[b, c]])

            if far and which == 0:
                products = [straight(0, half)] if b == 0 else [turned(0)]
            elif far:
                last = half - 1
                products = [turned(c) for c in range(half)] if b == last else [straight(last, half)]
            else:
                away = row if which == 0 else rows - 1 - row
                low = max(away, 1) if which == 0 else 0
                high = half if which == 0 else half - max(away, 1)
                products = []
                if low <= b < high:
                    products = [straight(b, high)] + [turned(c) for c in range(low, b)]
            value = partial_ref[place]
            for product in products:
                value = value + product
            if edge is not None:
                edge_ref[edge] = value
                continue
            value = finish(value, own_ref[row, :, cols(slot, 1)], mask_ref[row, slot], branch_ref[row])
            stats_ref[0:8] += fold(value * value)
            index = len(outs)
            staged[index] = value
            out = pltpu.make_async_copy(staged.at[index], out_ref.at[row, slot], out_sem.at[index])
            out.start()
            outs.append(out)
        for out in outs:
            out.wait()

    out_shape = [
        jax.ShapeDtypeStruct(square.shape, jnp.float32),
        jax.ShapeDtypeStruct((16, side), jnp.float32),
    ]
    if not far:
        out_shape.append(pltpu.VMEM((2 * half, side, side), jnp.float32))
    return pl.pallas_call(
        kernel,
        out_shape=tuple(out_shape),
        in_specs=[VMEM_ALL, SMEM, SMEM, ANY, VMEM_ALL, VMEM_ALL, VMEM_ALL],
        out_specs=(ANY,) + (VMEM_ALL,) * (len(out_shape) - 1),
        scratch_shapes=[
            pltpu.VMEM((finals, side, side), jnp.float32),
            pltpu.SemaphoreType.DMA((finals,)),
        ],
        input_output_aliases={3: 0},
        compiler_params=pltpu.CompilerParams(vmem_limit_bytes=(10 if far else 16) * 2**20),
        cost_estimate=pl.CostEstimate(
            flops=2 * (18 if far else 92) * side**3,
            transcendentals=0,
            bytes_accessed=4 * finals * side * side,
        ),
        name="halo_far" if far else "halo_near",
    )(
        in_vmem(own), mask, branch, square, in_vmem(partial), in_vmem(above), in_vmem(below)
    )


def in_vmem(value):
    return pltpu.with_memory_space_constraint(value, pltpu.VMEM)


def total_stats(stats, order, groups, members):
    def kernel(*refs):
        stat_refs = refs[: len(stats)]
        out_ref, mine, group, first, second, send_sem, first_sem, second_sem = refs[len(stats) :]
        g, m = lax.axis_index("grp"), lax.axis_index("mem")
        barrier = pltpu.get_barrier_semaphore()

        def greet_member(step, carry):
            other = lax.rem(m + step, members)
            pl.semaphore_signal(barrier, 1, device_id=(g, other), device_id_type=pl.DeviceIdType.MESH)
            return carry

        def greet_group(step, carry):
            other = lax.rem(g + step, groups)
            pl.semaphore_signal(barrier, 1, device_id=(other, m), device_id_type=pl.DeviceIdType.MESH)
            return carry

        lax.fori_loop(1, members, greet_member, 0)
        lax.fori_loop(1, groups, greet_group, 0)
        summed = stat_refs[0][...]
        for ref in stat_refs[1:]:
            summed = summed + ref[...]
        purity = jnp.sum(summed[0:8])
        trace = jnp.sum(summed[8:16])
        lane = lax.broadcasted_iota(jnp.int32, (8, 128), 1)
        mine[...] = jnp.where(lane == 0, trace, purity)
        pl.semaphore_wait(barrier, members + groups - 2)

        def exchange(source, slots, sems, me, count, device, offset):
            def copy(step):
                other = lax.rem(me + step, count)
                return pltpu.make_async_remote_copy(
                    source, slots.at[me], send_sem.at[offset + step], sems.at[me],
                    device_id=device(other), device_id_type=pl.DeviceIdType.MESH,
                )

            def arrival(step):
                other = lax.rem(me + step, count)
                return pltpu.make_async_remote_copy(
                    source, slots.at[other], send_sem.at[offset + step], sems.at[other],
                    device_id=device(other), device_id_type=pl.DeviceIdType.MESH,
                )

            def begin(step, carry):
                copy(step).start()
                return carry

            def end(step, carry):
                arrival(step).wait_recv()
                return carry

            def leave(step, carry):
                copy(step).wait_send()
                return carry

            lax.fori_loop(1, count, begin, 0)
            slots[me] = source[...]
            lax.fori_loop(1, count, end, 0)
            result = slots[0]
            for index in range(1, count):
                result = result + slots[index]
            return result, functools.partial(lax.fori_loop, 1, count, leave, 0)

        group_sum, leave_first = exchange(
            mine, first, first_sem, m, members, lambda other: (g, other), 0
        )
        group[...] = group_sum
        whole, leave_second = exchange(
            group, second, second_sem, g, groups, lambda other: (other, m), members
        )
        out_ref[...] = whole / order
        leave_first()
        leave_second()

    result = pl.pallas_call(
        kernel,
        out_shape=jax.ShapeDtypeStruct((8, 128), jnp.float32),
        in_specs=[VMEM_ALL] * len(stats),
        out_specs=VMEM_ALL,
        scratch_shapes=[
            pltpu.VMEM((8, 128), jnp.float32),
            pltpu.VMEM((8, 128), jnp.float32),
            pltpu.VMEM((members, 8, 128), jnp.float32),
            pltpu.VMEM((groups, 8, 128), jnp.float32),
            pltpu.SemaphoreType.DMA((members + groups,)),
            pltpu.SemaphoreType.DMA((members,)),
            pltpu.SemaphoreType.DMA((groups,)),
        ],
        compiler_params=pltpu.CompilerParams(
            collective_id=0, has_side_effects=True, vmem_limit_bytes=4 * 2**20
        ),
        name="total_stats",
    )(*stats)
    return result[0, 0:2]


def on_device(tiles, mask, branch, groups, members):
    rows, slots, side, _ = tiles.shape
    half = (slots - 1) // 2
    devices = groups * members
    lists = corner_lists(half)
    axes = ("grp", "mem")
    forward = [(index, index + 1) for index in range(devices - 1)]
    backward = [(index + 1, index) for index in range(devices - 1)]

    down_near, up_near, down_far, up_far = pack(tiles, mask, lists)
    above_near = lax.ppermute(down_near, axes, forward)
    below_near = lax.ppermute(up_near, axes, backward)
    above_far = lax.ppermute(down_far, axes, forward)
    below_far = lax.ppermute(up_far, axes, backward)

    square, local_stats, own, cross = local_part(tiles, mask, branch)
    square, near_stats, edge = halo_part(
        own, mask, branch, square, cross, above_near, below_near, lists, False
    )
    updated, far_stats = halo_part(
        own, mask, branch, square, edge, above_far, below_far, lists, True
    )
    order = float(rows * devices * side)
    traces = total_stats((local_stats, near_stats, far_stats), order, groups, members)
    return updated, traces


def solution(mesh):
    placed = (P(("grp", "mem"), None, None, None), P(("grp", "mem"), None), P(("grp", "mem")))
    return jax.shard_map(
        functools.partial(
            on_device, groups=mesh.shape["grp"], members=mesh.shape["mem"]
        ),
        mesh=mesh,
        in_specs=placed,
        out_specs=(P(("grp", "mem"), None, None, None), P()),
        check_vma=False,
    )
```

```python
import functools

import jax
import jax.numpy as jnp
from jax import lax
from jax.experimental import pallas as pl
from jax.experimental.pallas import tpu as pltpu
from jax.sharding import PartitionSpec as P


ANY = pl.BlockSpec(memory_space=pl.ANY)
SMEM = pl.BlockSpec(memory_space=pltpu.SMEM)
VMEM_ALL = pl.BlockSpec(memory_space=pltpu.VMEM)


def nn(left, right):
    return jnp.dot(left, right, preferred_element_type=jnp.float32)


def nt(left, right):
    return lax.dot_general(
        left, right, (((1,), (1,)), ((), ())), preferred_element_type=jnp.float32
    )


def finish(square, own, mask, branch):
    value = jnp.where(branch == 0, square, 2.0 * own.astype(jnp.float32) - square)
    return jnp.where(mask != 0, value, 0.0)


def fold(value):
    return jnp.sum(value.reshape(value.shape[0] // 8, 8, value.shape[1]), axis=0)


def corner_lists(half):
    upper_near = [(c, b) for b in range(1, half) for c in range(b, half)]
    upper_far = [(c, 0) for c in range(half)]
    lower_near = [(c, b) for b in range(half - 1) for c in range(b, half - 1)]
    lower_far = [(half - 1, b) for b in range(half)]
    return upper_near, upper_far, lower_near, lower_far


def triangle(count):
    return count * (count + 1) // 2


def layout(pairs, side):
    off = [pair for pair in pairs if pair[0] != pair[1]]
    diagonal = [pair for pair in pairs if pair[0] == pair[1]]
    first = len(off) * side
    last = first + len(diagonal) * (side // 2)
    spare = -(-len(diagonal) // 16) * 16
    return off, diagonal, first, last, spare


def block_places(small):
    row = lax.broadcasted_iota(jnp.int32, (small, small), 0)
    column = lax.broadcasted_iota(jnp.int32, (small, small), 1)
    return row, column


def pack(tiles, mask, lists):
    rows, slots, side, _ = tiles.shape
    half = (slots - 1) // 2
    small = side // 2
    upper_near, upper_far, lower_near, lower_far = lists
    order = (upper_near, lower_near, upper_far, lower_far)
    plans = [layout(pairs, side) for pairs in order]
    total = sum(len(pairs) for pairs in order)
    diagonals = sum(len(plan[1]) for plan in plans)

    def kernel(tiles_ref, mask_hbm, *refs):
        outs, (held, mask_ref, in_sem, mask_sem) = refs[:4], refs[4:]
        mask_copy = pltpu.make_async_copy(mask_hbm, mask_ref, mask_sem)
        mask_copy.start()
        work = []
        for which, (off, diagonal, first, _, _) in enumerate(plans):
            for index, (c, b) in enumerate(off + diagonal):
                row = rows - half + c if which % 2 == 0 else c
                slot = b - c + half
                if c != b:
                    target = outs[which].at[pl.ds(index * side, side)]
                else:
                    target = held.at[sum(item[4] is not None for item in work)]
                copy = pltpu.make_async_copy(
                    tiles_ref.at[row, slot], target, in_sem.at[len(work)]
                )
                copy.start()
                work.append((copy, row, slot, target, index - len(off) if c == b else None, which))
        mask_copy.wait()
        r, c = block_places(small)
        place = 0
        lines = {}
        for copy, row, slot, target, index, which in work:
            copy.wait()

            @pl.when(mask_ref[row, slot] == 0)
            def _():
                target[...] = jnp.zeros((side, side), tiles.dtype)

            if index is None:
                continue
            first, last, spare = plans[which][2:]
            start = first + index * small
            top = held[place, 0:small, 0:small].astype(jnp.float32)
            bottom = held[place, small:side, small:side].astype(jnp.float32)
            outs[which][start : start + small, 0:small] = jnp.where(r >= c, top, bottom).astype(
                tiles.dtype
            )
            outs[which][start : start + small, small:side] = held[place, 0:small, small:side]
            line = jnp.sum(jnp.where(r == c, bottom, 0.0), axis=0, keepdims=True)
            at = lax.broadcasted_iota(jnp.int32, (spare, small), 0) == index
            before = lines.get(which, jnp.zeros((spare, small), jnp.float32))
            lines[which] = jnp.where(at, line, before)
            place += 1
        for which, value in lines.items():
            last, spare = plans[which][3:]
            value = value.astype(tiles.dtype)
            outs[which][last : last + spare, 0:small] = value
            outs[which][last : last + spare, small:side] = value

    return pl.pallas_call(
        kernel,
        out_shape=tuple(
            pltpu.VMEM((plan[3] + plan[4], side), tiles.dtype) for plan in plans
        ),
        in_specs=[pl.BlockSpec(memory_space=pltpu.HBM)] * 2,
        out_specs=(VMEM_ALL,) * 4,
        scratch_shapes=[
            pltpu.VMEM((diagonals, side, side), tiles.dtype),
            pltpu.SMEM(mask.shape, jnp.int32),
            pltpu.SemaphoreType.DMA((total,)),
            pltpu.SemaphoreType.DMA,
        ],
        compiler_params=pltpu.CompilerParams(vmem_limit_bytes=8 * 2**20),
        cost_estimate=pl.CostEstimate(
            flops=0, transcendentals=0, bytes_accessed=4 * total * side * side
        ),
        name="pack",
    )(in_hbm(tiles), in_hbm(mask))


def local_part(tiles, mask, branch):
    rows, slots, side, _ = tiles.shape
    half = (slots - 1) // 2
    corner = triangle(half)

    def kernel(
        tiles_ref, mask_ref, branch_ref, out_ref, stats_ref, own, cross,
        left, right, staged, in_sem, out_sem,
    ):
        def cols(start, count):
            return pl.ds(start * side, count * side)

        copies = []
        for row in range(rows):
            for slot in range(slots):
                copies.append(
                    pltpu.make_async_copy(
                        tiles_ref.at[row, slot], own.at[row, :, cols(slot, 1)], in_sem
                    )
                )
        for copy in copies:
            copy.start()
        stats_ref[...] = jnp.zeros_like(stats_ref)
        for copy in copies:
            copy.wait()
        for row in range(rows):
            for slot in range(slots):

                @pl.when(mask_ref[row, slot] == 0)
                def _():
                    own[row, :, cols(slot, 1)] = jnp.zeros((side, side), own.dtype)

        for k in range(half):
            for b in range(k, half):
                left[cols(k, 1), cols(b, 1)] = own[k, :, cols(b - k, 1)]
        for k in range(half):
            row = rows - half + k
            for b in range(k + 1):
                right[cols(k, 1), cols(b, 1)] = own[row, :, cols(rows + b - row + half, 1)]

        def out_copy(row, column):
            return pltpu.make_async_copy(
                staged.at[row, column], out_ref.at[row, column - row + half], out_sem
            )

        def settle(row, column, square):
            slot = column - row + half
            start = pl.multiple_of(slot * side, side)
            value = finish(
                square, own[row, :, pl.ds(start, side)], mask_ref[row, slot], branch_ref[row]
            )
            staged[row, column] = value
            stats_ref[0:8] += fold(value * value)
            out_copy(row, column).start()
            return value

        @pl.loop(0, rows)
        def _(row):
            for d in range(half + 1):

                @pl.when(row + d < rows)
                def _():
                    square = nt(
                        own[row, :, cols(d, slots - d)], own[row + d, :, cols(0, slots - d)]
                    )
                    value = settle(row, row + d, square)
                    if d == 0:
                        on = lax.broadcasted_iota(jnp.int32, value.shape, 0) == (
                            lax.broadcasted_iota(jnp.int32, value.shape, 1)
                        )
                        stats_ref[8:16] += fold(jnp.where(on, value, 0.0))
                    else:
                        settle(row + d, row, square.T)

            for b in range(half):
                @pl.when(row <= b)
                def _():
                    start = pl.multiple_of((half - row) * side, side)
                    cross[triangle(b) + row] = nn(
                        own[row, :, pl.ds(start, (b + 1) * side)],
                        left[cols(0, b + 1), cols(b, 1)],
                    )

                @pl.when(row >= rows - half + b)
                def _():
                    first = rows - half + b
                    start = pl.multiple_of((first - row + half) * side, side)
                    cross[corner + triangle(half - 1 - b) + rows - 1 - row] = nn(
                        own[row, :, pl.ds(start, (half - b) * side)],
                        right[cols(b, half - b), cols(b, 1)],
                    )

        for row in range(rows):
            for column in range(rows):
                if abs(row - column) <= half:
                    out_copy(row, column).wait()

    matmuls = 300
    return pl.pallas_call(
        kernel,
        out_shape=(
            jax.ShapeDtypeStruct(tiles.shape, jnp.float32),
            jax.ShapeDtypeStruct((16, side), jnp.float32),
            pltpu.VMEM((rows, side, slots * side), tiles.dtype),
            pltpu.VMEM((2 * corner, side, side), jnp.float32),
        ),
        in_specs=[pl.BlockSpec(memory_space=pltpu.HBM), SMEM, SMEM],
        out_specs=(ANY, VMEM_ALL, VMEM_ALL, VMEM_ALL),
        scratch_shapes=[
            pltpu.VMEM((half * side, half * side), tiles.dtype),
            pltpu.VMEM((half * side, half * side), tiles.dtype),
            pltpu.VMEM((rows, rows, side, side), jnp.float32),
            pltpu.SemaphoreType.DMA,
            pltpu.SemaphoreType.DMA,
        ],
        compiler_params=pltpu.CompilerParams(vmem_limit_bytes=22 * 2**20),
        cost_estimate=pl.CostEstimate(
            flops=2 * matmuls * side**3, transcendentals=0, bytes_accessed=6 * tiles.size
        ),
        name="local_part",
    )(in_hbm(tiles), mask, branch)


def halo_part(own, mask, branch, square, partial, above, below, lists, far):
    rows, side, width = own.shape
    slots = width // side
    half = (slots - 1) // 2
    corner = triangle(half)
    upper_near, upper_far, lower_near, lower_far = lists
    small = side // 2
    chunks = (upper_far, lower_far) if far else (upper_near, lower_near)

    jobs = []
    if far:
        jobs += [(0, 0, b, b, b, None) for b in range(half)]
        jobs += [(rows - 1, 1, b, half + 1 + b, half + b, None) for b in range(half)]
    else:
        for a in range(half):
            for b in range(a, half):
                jobs.append((a, 0, b, b - a, triangle(b) + a, None if a else b))
            row = rows - 1 - a
            for b in range(half - a):
                place = corner + triangle(half - 1 - b) + a
                jobs.append((row, 1, b, rows + b - row + half, place, None if a else half + b))
    finals = sum(job[5] is None for job in jobs)

    def kernel(own_ref, mask_ref, branch_ref, square_ref, partial_ref, above_ref, below_ref, *refs):
        if far:
            out_ref, stats_ref, held, staged, out_sem = refs
        else:
            out_ref, stats_ref, edge_ref, held, staged, out_sem = refs

        def cols(start, count):
            return pl.ds(start * side, count * side)

        r, c = block_places(small)
        for which, (source, pairs) in enumerate(zip((above_ref, below_ref), chunks)):
            off, diagonal, first, last, _ = layout(pairs, side)
            for index, (i, j) in enumerate(off):
                held[which, cols(i, 1), cols(j, 1)] = source[index * side : (index + 1) * side]
            for index, (i, _) in enumerate(diagonal):
                low, mid, high = i * side, i * side + small, (i + 1) * side
                start = first + index * small
                mixed = source[start : start + small, 0:small].astype(jnp.float32)
                flipped = mixed.T
                line = source[last : last + 16, 0:small].astype(jnp.float32)[index : index + 1]
                bottom = jnp.where(r == c, line, jnp.where(r < c, mixed, flipped))
                side_block = source[start : start + small, small:side]
                held[which, low:mid, low:mid] = jnp.where(r >= c, mixed, flipped).astype(own.dtype)
                held[which, low:mid, mid:high] = side_block
                held[which, mid:high, low:mid] = (
                    side_block.astype(jnp.float32).T.astype(own.dtype)
                )
                held[which, mid:high, mid:high] = bottom.astype(own.dtype)

        outs = []
        stats_ref[...] = jnp.zeros_like(stats_ref)
        for row, which, b, slot, place, edge in jobs:
            base = -row if which == 0 else rows - row + half

            def straight(low, high):
                return nn(
                    own_ref[row, :, cols(base + low, high - low)],
                    held[which, cols(low, high - low), cols(b, 1)],
                )

            def turned(low, high):
                return nt(
                    own_ref[row, :, cols(base + low, high - low)],
                    held[which, cols(b, 1), cols(low, high - low)],
                )

            if far and which == 0:
                products = [straight(0, half)] if b == 0 else [turned(0, 1)]
            elif far:
                last = half - 1
                products = [turned(0, half)] if b == last else [straight(last, half)]
            else:
                away = row if which == 0 else rows - 1 - row
                low = max(away, 1) if which == 0 else 0
                high = half if which == 0 else half - max(away, 1)
                products = []
                if low <= b < high:
                    products = [straight(b, high)]
                    if b > low:
                        products.append(turned(low, b))
            value = partial_ref[place]
            for product in products:
                value = value + product
            if edge is not None:
                edge_ref[edge] = value
                continue
            value = finish(value, own_ref[row, :, cols(slot, 1)], mask_ref[row, slot], branch_ref[row])
            stats_ref[0:8] += fold(value * value)
            index = len(outs)
            staged[index] = value
            out = pltpu.make_async_copy(staged.at[index], out_ref.at[row, slot], out_sem.at[index])
            out.start()
            outs.append(out)
        for out in outs:
            out.wait()

    out_shape = [
        jax.ShapeDtypeStruct(square.shape, jnp.float32),
        jax.ShapeDtypeStruct((16, side), jnp.float32),
    ]
    if not far:
        out_shape.append(pltpu.VMEM((2 * half, side, side), jnp.float32))
    return pl.pallas_call(
        kernel,
        out_shape=tuple(out_shape),
        in_specs=[VMEM_ALL, SMEM, SMEM, ANY, VMEM_ALL, VMEM_ALL, VMEM_ALL],
        out_specs=(ANY,) + (VMEM_ALL,) * (len(out_shape) - 1),
        scratch_shapes=[
            pltpu.VMEM((2, half * side, half * side), own.dtype),
            pltpu.VMEM((finals, side, side), jnp.float32),
            pltpu.SemaphoreType.DMA((finals,)),
        ],
        input_output_aliases={3: 0},
        compiler_params=pltpu.CompilerParams(vmem_limit_bytes=(16 if far else 20) * 2**20),
        cost_estimate=pl.CostEstimate(
            flops=2 * (18 if far else 92) * side**3,
            transcendentals=0,
            bytes_accessed=4 * finals * side * side,
        ),
        name="halo_far" if far else "halo_near",
    )(
        in_vmem(own), mask, branch, square, in_vmem(partial), in_vmem(above), in_vmem(below)
    )


def in_hbm(value):
    return pltpu.with_memory_space_constraint(value, pltpu.HBM)


def in_vmem(value):
    return pltpu.with_memory_space_constraint(value, pltpu.VMEM)


def total_stats(stats, order, groups, members):
    def kernel(*refs):
        stat_refs = refs[: len(stats)]
        out_ref, mine, group, first, second, send_sem, first_sem, second_sem = refs[len(stats) :]
        g, m = lax.axis_index("grp"), lax.axis_index("mem")
        barrier = pltpu.get_barrier_semaphore()

        def greet_member(step, carry):
            other = lax.rem(m + step, members)
            pl.semaphore_signal(barrier, 1, device_id=(g, other), device_id_type=pl.DeviceIdType.MESH)
            return carry

        def greet_group(step, carry):
            other = lax.rem(g + step, groups)
            pl.semaphore_signal(barrier, 1, device_id=(other, m), device_id_type=pl.DeviceIdType.MESH)
            return carry

        lax.fori_loop(1, members, greet_member, 0)
        lax.fori_loop(1, groups, greet_group, 0)
        summed = stat_refs[0][...]
        for ref in stat_refs[1:]:
            summed = summed + ref[...]
        purity = jnp.sum(summed[0:8])
        trace = jnp.sum(summed[8:16])
        lane = lax.broadcasted_iota(jnp.int32, (8, 128), 1)
        mine[...] = jnp.where(lane == 0, trace, purity)
        pl.semaphore_wait(barrier, members + groups - 2)

        def exchange(source, slots, sems, me, count, device, offset):
            def copy(step):
                other = lax.rem(me + step, count)
                return pltpu.make_async_remote_copy(
                    source, slots.at[me], send_sem.at[offset + step], sems.at[me],
                    device_id=device(other), device_id_type=pl.DeviceIdType.MESH,
                )

            def arrival(step):
                other = lax.rem(me + step, count)
                return pltpu.make_async_remote_copy(
                    source, slots.at[other], send_sem.at[offset + step], sems.at[other],
                    device_id=device(other), device_id_type=pl.DeviceIdType.MESH,
                )

            def begin(step, carry):
                copy(step).start()
                return carry

            def end(step, carry):
                arrival(step).wait_recv()
                return carry

            def leave(step, carry):
                copy(step).wait_send()
                return carry

            lax.fori_loop(1, count, begin, 0)
            slots[me] = source[...]
            lax.fori_loop(1, count, end, 0)
            result = slots[0]
            for index in range(1, count):
                result = result + slots[index]
            return result, functools.partial(lax.fori_loop, 1, count, leave, 0)

        group_sum, leave_first = exchange(
            mine, first, first_sem, m, members, lambda other: (g, other), 0
        )
        group[...] = group_sum
        whole, leave_second = exchange(
            group, second, second_sem, g, groups, lambda other: (other, m), members
        )
        out_ref[...] = whole / order
        leave_first()
        leave_second()

    result = pl.pallas_call(
        kernel,
        out_shape=jax.ShapeDtypeStruct((8, 128), jnp.float32),
        in_specs=[VMEM_ALL] * len(stats),
        out_specs=VMEM_ALL,
        scratch_shapes=[
            pltpu.VMEM((8, 128), jnp.float32),
            pltpu.VMEM((8, 128), jnp.float32),
            pltpu.VMEM((members, 8, 128), jnp.float32),
            pltpu.VMEM((groups, 8, 128), jnp.float32),
            pltpu.SemaphoreType.DMA((members + groups,)),
            pltpu.SemaphoreType.DMA((members,)),
            pltpu.SemaphoreType.DMA((groups,)),
        ],
        compiler_params=pltpu.CompilerParams(
            collective_id=0, has_side_effects=True, vmem_limit_bytes=4 * 2**20
        ),
        name="total_stats",
    )(*stats)
    return result[0, 0:2]


def on_device(tiles, mask, branch, groups, members):
    rows, slots, side, _ = tiles.shape
    half = (slots - 1) // 2
    devices = groups * members
    lists = corner_lists(half)
    axes = ("grp", "mem")
    forward = [(index, index + 1) for index in range(devices - 1)]
    backward = [(index + 1, index) for index in range(devices - 1)]

    down_near, up_near, down_far, up_far = pack(tiles, mask, lists)
    above_near = lax.ppermute(down_near, axes, forward)
    below_near = lax.ppermute(up_near, axes, backward)
    above_far = lax.ppermute(down_far, axes, forward)
    below_far = lax.ppermute(up_far, axes, backward)

    square, local_stats, own, cross = local_part(tiles, mask, branch)
    square, near_stats, edge = halo_part(
        own, mask, branch, square, cross, above_near, below_near, lists, False
    )
    updated, far_stats = halo_part(
        own, mask, branch, square, edge, above_far, below_far, lists, True
    )
    order = float(rows * devices * side)
    traces = total_stats((local_stats, near_stats, far_stats), order, groups, members)
    return updated, traces


def solution(mesh):
    placed = (P(("grp", "mem"), None, None, None), P(("grp", "mem"), None), P(("grp", "mem")))
    return jax.shard_map(
        functools.partial(
            on_device, groups=mesh.shape["grp"], members=mesh.shape["mem"]
        ),
        mesh=mesh,
        in_specs=placed,
        out_specs=(P(("grp", "mem"), None, None, None), P()),
        check_vma=False,
    )
```

```python
import functools

import jax
import jax.numpy as jnp
from jax import lax
from jax.experimental import pallas as pl
from jax.experimental.pallas import tpu as pltpu
from jax.sharding import PartitionSpec as P


ANY = pl.BlockSpec(memory_space=pl.ANY)
SMEM = pl.BlockSpec(memory_space=pltpu.SMEM)
VMEM_ALL = pl.BlockSpec(memory_space=pltpu.VMEM)


def nn(left, right):
    return jnp.dot(left, right, preferred_element_type=jnp.float32)


def nt(left, right):
    return lax.dot_general(
        left, right, (((1,), (1,)), ((), ())), preferred_element_type=jnp.float32
    )


def weights(mask, branch):
    keep = mask.astype(jnp.float32)
    return jnp.where(branch == 0, 0.0, 2.0 * keep), jnp.where(branch == 0, keep, -keep)


def finish(square, own, scale):
    return scale[0] * own.astype(jnp.float32) + scale[1] * square


def fold(value):
    return jnp.sum(value.reshape(value.shape[0] // 8, 8, value.shape[1]), axis=0)


def corner_lists(half):
    upper_near = [(c, b) for b in range(1, half) for c in range(b, half)]
    upper_far = [(c, 0) for c in range(half)]
    lower_near = [(c, b) for b in range(half - 1) for c in range(b, half - 1)]
    lower_far = [(half - 1, b) for b in range(half)]
    return upper_near, upper_far, lower_near, lower_far


def triangle(count):
    return count * (count + 1) // 2


def layout(pairs, side):
    off = [pair for pair in pairs if pair[0] != pair[1]]
    diagonal = [pair for pair in pairs if pair[0] == pair[1]]
    first = len(off) * side
    last = first + len(diagonal) * (side // 2)
    spare = -(-len(diagonal) // 16) * 16
    return off, diagonal, first, last, spare


def block_places(small):
    row = lax.broadcasted_iota(jnp.int32, (small, small), 0)
    column = lax.broadcasted_iota(jnp.int32, (small, small), 1)
    return row, column


def pack(tiles, mask, lists):
    rows, slots, side, _ = tiles.shape
    half = (slots - 1) // 2
    small = side // 2
    upper_near, upper_far, lower_near, lower_far = lists
    order = (upper_near, lower_near, upper_far, lower_far)
    plans = [layout(pairs, side) for pairs in order]
    total = sum(len(pairs) for pairs in order)
    diagonals = sum(len(plan[1]) for plan in plans)

    def kernel(tiles_ref, mask_hbm, *refs):
        outs, (held, mask_ref, in_sem, mask_sem) = refs[:4], refs[4:]
        mask_copy = pltpu.make_async_copy(mask_hbm, mask_ref, mask_sem)
        mask_copy.start()
        work = []
        for which, (off, diagonal, first, _, _) in enumerate(plans):
            for index, (c, b) in enumerate(off + diagonal):
                row = rows - half + c if which % 2 == 0 else c
                slot = b - c + half
                if c != b:
                    target = outs[which].at[pl.ds(index * side, side)]
                else:
                    target = held.at[sum(item[4] is not None for item in work)]
                copy = pltpu.make_async_copy(
                    tiles_ref.at[row, slot], target, in_sem.at[len(work)]
                )
                copy.start()
                work.append((copy, row, slot, target, index - len(off) if c == b else None, which))
        mask_copy.wait()
        r, c = block_places(small)
        place = 0
        lines = {}
        for copy, row, slot, target, index, which in work:
            copy.wait()

            @pl.when(mask_ref[row, slot] == 0)
            def _():
                target[...] = jnp.zeros((side, side), tiles.dtype)

            if index is None:
                continue
            first, last, spare = plans[which][2:]
            start = first + index * small
            top = held[place, 0:small, 0:small].astype(jnp.float32)
            bottom = held[place, small:side, small:side].astype(jnp.float32)
            outs[which][start : start + small, 0:small] = jnp.where(r >= c, top, bottom).astype(
                tiles.dtype
            )
            outs[which][start : start + small, small:side] = held[place, 0:small, small:side]
            line = jnp.sum(jnp.where(r == c, bottom, 0.0), axis=0, keepdims=True)
            at = lax.broadcasted_iota(jnp.int32, (spare, small), 0) == index
            before = lines.get(which, jnp.zeros((spare, small), jnp.float32))
            lines[which] = jnp.where(at, line, before)
            place += 1
        for which, value in lines.items():
            last, spare = plans[which][3:]
            value = value.astype(tiles.dtype)
            outs[which][last : last + spare, 0:small] = value
            outs[which][last : last + spare, small:side] = value

    return pl.pallas_call(
        kernel,
        out_shape=tuple(
            pltpu.VMEM((plan[3] + plan[4], side), tiles.dtype) for plan in plans
        ),
        in_specs=[pl.BlockSpec(memory_space=pltpu.HBM)] * 2,
        out_specs=(VMEM_ALL,) * 4,
        scratch_shapes=[
            pltpu.VMEM((diagonals, side, side), tiles.dtype),
            pltpu.SMEM(mask.shape, jnp.int32),
            pltpu.SemaphoreType.DMA((total,)),
            pltpu.SemaphoreType.DMA,
        ],
        compiler_params=pltpu.CompilerParams(vmem_limit_bytes=8 * 2**20),
        cost_estimate=pl.CostEstimate(
            flops=0, transcendentals=0, bytes_accessed=4 * total * side * side
        ),
        name="pack",
    )(in_hbm(tiles), in_hbm(mask))


def local_part(tiles, mask, branch):
    rows, slots, side, _ = tiles.shape
    half = (slots - 1) // 2
    corner = triangle(half)
    small = side // 2

    def kernel(
        tiles_ref, mask_ref, branch_ref, out_ref, stats_ref, own, cross,
        left, right, staged, in_sem, out_sem,
    ):
        def cols(start, count):
            return pl.ds(start * side, count * side)

        def load(row, slot):
            return pltpu.make_async_copy(
                tiles_ref.at[row, slot], own.at[row, :, cols(slot, 1)], in_sem.at[row]
            )

        for row in range(rows):
            for slot in range(slots):
                load(row, slot).start()
        stats_ref[...] = jnp.zeros_like(stats_ref)
        for row in range(rows):
            for slot in range(slots):
                load(row, slot).wait()
            for slot in range(slots):

                @pl.when(mask_ref[row, slot] == 0)
                def _():
                    own[row, :, cols(slot, 1)] = jnp.zeros((side, side), own.dtype)

            if row < half:
                for b in range(row, half):
                    left[cols(row, 1), cols(b, 1)] = own[row, :, cols(b - row, 1)]
            k = row - (rows - half)
            if k >= 0:
                for b in range(k + 1):
                    right[cols(k, 1), cols(b, 1)] = own[row, :, cols(rows + b - row + half, 1)]

        def out_copy(row, column):
            return pltpu.make_async_copy(
                staged.at[row, column], out_ref.at[row, column - row + half], out_sem
            )

        def own_block(row, slot, top, start):
            lanes = pl.ds(pl.multiple_of(slot * side + start, small), small)
            return own[row, top : top + small, lanes]

        @pl.loop(0, rows)
        def _(row):
            for d in range(half + 1):

                @pl.when(row + d < rows)
                def _():
                    other = row + d
                    staged[row, other] = nt(
                        own[row, :, cols(d, slots - d)], own[other, :, cols(0, slots - d)]
                    )
                    scale = weights(mask_ref[row, half + d], branch_ref[row])
                    other_scale = weights(mask_ref[other, half - d], branch_ref[other])
                    purity = jnp.zeros((8, small), jnp.float32)
                    trace = jnp.zeros((8, small), jnp.float32)
                    for top in range(0, side, small):
                        for start in range(0, side, small):
                            down, across = slice(top, top + small), slice(start, start + small)
                            raw = staged[row, other, down, across]
                            if d:
                                value = finish(
                                    raw.T, own_block(other, half - d, start, top), other_scale
                                )
                                staged[other, row, across, down] = value
                                purity = purity + fold(value * value)
                            value = finish(raw, own_block(row, half + d, top, start), scale)
                            staged[row, other, down, across] = value
                            purity = purity + fold(value * value)
                            if d == 0 and top == start:
                                r, c = block_places(small)
                                trace = trace + fold(jnp.where(r == c, value, 0.0))
                    out_copy(row, other).start()
                    if d:
                        out_copy(other, row).start()
                    else:
                        stats_ref[8:16, 0:small] += trace
                    stats_ref[0:8, 0:small] += purity

            for b in range(half):
                @pl.when(row <= b)
                def _():
                    start = pl.multiple_of((half - row) * side, side)
                    cross[triangle(b) + row] = nn(
                        own[row, :, pl.ds(start, (b + 1) * side)],
                        left[cols(0, b + 1), cols(b, 1)],
                    )

                @pl.when(row >= rows - half + b)
                def _():
                    first = rows - half + b
                    start = pl.multiple_of((first - row + half) * side, side)
                    cross[corner + triangle(half - 1 - b) + rows - 1 - row] = nn(
                        own[row, :, pl.ds(start, (half - b) * side)],
                        right[cols(b, half - b), cols(b, 1)],
                    )

        for row in range(rows):
            for column in range(rows):
                if abs(row - column) <= half:
                    out_copy(row, column).wait()

    matmuls = 300
    return pl.pallas_call(
        kernel,
        out_shape=(
            jax.ShapeDtypeStruct(tiles.shape, jnp.float32),
            jax.ShapeDtypeStruct((16, side), jnp.float32),
            pltpu.VMEM((rows, side, slots * side), tiles.dtype),
            pltpu.VMEM((2 * corner, side, side), jnp.float32),
        ),
        in_specs=[pl.BlockSpec(memory_space=pltpu.HBM), SMEM, SMEM],
        out_specs=(ANY, VMEM_ALL, VMEM_ALL, VMEM_ALL),
        scratch_shapes=[
            pltpu.VMEM((half * side, half * side), tiles.dtype),
            pltpu.VMEM((half * side, half * side), tiles.dtype),
            pltpu.VMEM((rows, rows, side, side), jnp.float32),
            pltpu.SemaphoreType.DMA((rows,)),
            pltpu.SemaphoreType.DMA,
        ],
        compiler_params=pltpu.CompilerParams(vmem_limit_bytes=22 * 2**20),
        cost_estimate=pl.CostEstimate(
            flops=2 * matmuls * side**3, transcendentals=0, bytes_accessed=6 * tiles.size
        ),
        name="local_part",
    )(in_hbm(tiles), mask, branch)


def halo_part(own, mask, branch, square, partial, above, below, lists, far):
    rows, side, width = own.shape
    slots = width // side
    half = (slots - 1) // 2
    corner = triangle(half)
    upper_near, upper_far, lower_near, lower_far = lists
    small = side // 2
    chunks = (upper_far, lower_far) if far else (upper_near, lower_near)

    jobs = []
    if far:
        jobs += [(0, 0, b, b, b, None) for b in range(half)]
        jobs += [(rows - 1, 1, b, half + 1 + b, half + b, None) for b in range(half)]
    else:
        for a in range(half):
            for b in range(a, half):
                jobs.append((a, 0, b, b - a, triangle(b) + a, None if a else b))
            row = rows - 1 - a
            for b in range(half - a):
                place = corner + triangle(half - 1 - b) + a
                jobs.append((row, 1, b, rows + b - row + half, place, None if a else half + b))
    finals = sum(job[5] is None for job in jobs)

    def kernel(own_ref, mask_ref, branch_ref, square_ref, partial_ref, above_ref, below_ref, *refs):
        if far:
            out_ref, stats_ref, held, staged, out_sem = refs
        else:
            out_ref, stats_ref, edge_ref, held, staged, out_sem = refs

        def cols(start, count):
            return pl.ds(start * side, count * side)

        r, c = block_places(small)
        for which, (source, pairs) in enumerate(zip((above_ref, below_ref), chunks)):
            off, diagonal, first, last, _ = layout(pairs, side)
            for index, (i, j) in enumerate(off):
                held[which, cols(i, 1), cols(j, 1)] = source[index * side : (index + 1) * side]
            for index, (i, _) in enumerate(diagonal):
                low, mid, high = i * side, i * side + small, (i + 1) * side
                start = first + index * small
                mixed = source[start : start + small, 0:small].astype(jnp.float32)
                flipped = mixed.T
                line = source[last : last + 16, 0:small].astype(jnp.float32)[index : index + 1]
                bottom = jnp.where(r == c, line, jnp.where(r < c, mixed, flipped))
                side_block = source[start : start + small, small:side]
                held[which, low:mid, low:mid] = jnp.where(r >= c, mixed, flipped).astype(own.dtype)
                held[which, low:mid, mid:high] = side_block
                held[which, mid:high, low:mid] = (
                    side_block.astype(jnp.float32).T.astype(own.dtype)
                )
                held[which, mid:high, mid:high] = bottom.astype(own.dtype)

        outs = []
        stats_ref[...] = jnp.zeros_like(stats_ref)
        for row, which, b, slot, place, edge in jobs:
            base = -row if which == 0 else rows - row + half

            def straight(low, high):
                return nn(
                    own_ref[row, :, cols(base + low, high - low)],
                    held[which, cols(low, high - low), cols(b, 1)],
                )

            def turned(low, high):
                return nt(
                    own_ref[row, :, cols(base + low, high - low)],
                    held[which, cols(b, 1), cols(low, high - low)],
                )

            if far and which == 0:
                products = [straight(0, half)] if b == 0 else [turned(0, 1)]
            elif far:
                last = half - 1
                products = [turned(0, half)] if b == last else [straight(last, half)]
            else:
                away = row if which == 0 else rows - 1 - row
                low = max(away, 1) if which == 0 else 0
                high = half if which == 0 else half - max(away, 1)
                products = []
                if low <= b < high:
                    products = [straight(b, high)]
                    if b > low:
                        products.append(turned(low, b))
            value = partial_ref[place]
            for product in products:
                value = value + product
            if edge is not None:
                edge_ref[edge] = value
                continue
            index = len(outs)
            staged[index] = value
            scale = weights(mask_ref[row, slot], branch_ref[row])
            purity = jnp.zeros((8, side), jnp.float32)
            for top in range(0, side, small // 2):
                down = slice(top, top + small // 2)
                value = finish(staged[index, down], own_ref[row, down, cols(slot, 1)], scale)
                staged[index, down] = value
                purity = purity + fold(value * value)
            stats_ref[0:8] += purity
            out = pltpu.make_async_copy(staged.at[index], out_ref.at[row, slot], out_sem.at[index])
            out.start()
            outs.append(out)
        for out in outs:
            out.wait()

    out_shape = [
        jax.ShapeDtypeStruct(square.shape, jnp.float32),
        jax.ShapeDtypeStruct((16, side), jnp.float32),
    ]
    if not far:
        out_shape.append(pltpu.VMEM((2 * half, side, side), jnp.float32))
    return pl.pallas_call(
        kernel,
        out_shape=tuple(out_shape),
        in_specs=[VMEM_ALL, SMEM, SMEM, ANY, VMEM_ALL, VMEM_ALL, VMEM_ALL],
        out_specs=(ANY,) + (VMEM_ALL,) * (len(out_shape) - 1),
        scratch_shapes=[
            pltpu.VMEM((2, half * side, half * side), own.dtype),
            pltpu.VMEM((finals, side, side), jnp.float32),
            pltpu.SemaphoreType.DMA((finals,)),
        ],
        input_output_aliases={3: 0},
        compiler_params=pltpu.CompilerParams(vmem_limit_bytes=(16 if far else 20) * 2**20),
        cost_estimate=pl.CostEstimate(
            flops=2 * (18 if far else 92) * side**3,
            transcendentals=0,
            bytes_accessed=4 * finals * side * side,
        ),
        name="halo_far" if far else "halo_near",
    )(
        in_vmem(own), mask, branch, square, in_vmem(partial), in_vmem(above), in_vmem(below)
    )


def in_hbm(value):
    return pltpu.with_memory_space_constraint(value, pltpu.HBM)


def in_vmem(value):
    return pltpu.with_memory_space_constraint(value, pltpu.VMEM)


def total_stats(stats, order, groups, members):
    def kernel(*refs):
        stat_refs = refs[: len(stats)]
        out_ref, mine, group, first, second, send_sem, first_sem, second_sem = refs[len(stats) :]
        g, m = lax.axis_index("grp"), lax.axis_index("mem")
        barrier = pltpu.get_barrier_semaphore()

        def greet_member(step, carry):
            other = lax.rem(m + step, members)
            pl.semaphore_signal(barrier, 1, device_id=(g, other), device_id_type=pl.DeviceIdType.MESH)
            return carry

        def greet_group(step, carry):
            other = lax.rem(g + step, groups)
            pl.semaphore_signal(barrier, 1, device_id=(other, m), device_id_type=pl.DeviceIdType.MESH)
            return carry

        lax.fori_loop(1, members, greet_member, 0)
        lax.fori_loop(1, groups, greet_group, 0)
        summed = stat_refs[0][...]
        for ref in stat_refs[1:]:
            summed = summed + ref[...]
        purity = jnp.sum(summed[0:8])
        trace = jnp.sum(summed[8:16])
        lane = lax.broadcasted_iota(jnp.int32, (8, 128), 1)
        mine[...] = jnp.where(lane == 0, trace, purity)
        pl.semaphore_wait(barrier, members + groups - 2)

        def exchange(source, slots, sems, me, count, device, offset):
            def copy(step):
                other = lax.rem(me + step, count)
                return pltpu.make_async_remote_copy(
                    source, slots.at[me], send_sem.at[offset + step], sems.at[me],
                    device_id=device(other), device_id_type=pl.DeviceIdType.MESH,
                )

            def arrival(step):
                other = lax.rem(me + step, count)
                return pltpu.make_async_remote_copy(
                    source, slots.at[other], send_sem.at[offset + step], sems.at[other],
                    device_id=device(other), device_id_type=pl.DeviceIdType.MESH,
                )

            def begin(step, carry):
                copy(step).start()
                return carry

            def end(step, carry):
                arrival(step).wait_recv()
                return carry

            def leave(step, carry):
                copy(step).wait_send()
                return carry

            lax.fori_loop(1, count, begin, 0)
            slots[me] = source[...]
            lax.fori_loop(1, count, end, 0)
            result = slots[0]
            for index in range(1, count):
                result = result + slots[index]
            return result, functools.partial(lax.fori_loop, 1, count, leave, 0)

        group_sum, leave_first = exchange(
            mine, first, first_sem, m, members, lambda other: (g, other), 0
        )
        group[...] = group_sum
        whole, leave_second = exchange(
            group, second, second_sem, g, groups, lambda other: (other, m), members
        )
        out_ref[...] = whole / order
        leave_first()
        leave_second()

    result = pl.pallas_call(
        kernel,
        out_shape=jax.ShapeDtypeStruct((8, 128), jnp.float32),
        in_specs=[VMEM_ALL] * len(stats),
        out_specs=VMEM_ALL,
        scratch_shapes=[
            pltpu.VMEM((8, 128), jnp.float32),
            pltpu.VMEM((8, 128), jnp.float32),
            pltpu.VMEM((members, 8, 128), jnp.float32),
            pltpu.VMEM((groups, 8, 128), jnp.float32),
            pltpu.SemaphoreType.DMA((members + groups,)),
            pltpu.SemaphoreType.DMA((members,)),
            pltpu.SemaphoreType.DMA((groups,)),
        ],
        compiler_params=pltpu.CompilerParams(
            collective_id=0, has_side_effects=True, vmem_limit_bytes=4 * 2**20
        ),
        name="total_stats",
    )(*stats)
    return result[0, 0:2]


def on_device(tiles, mask, branch, groups, members):
    rows, slots, side, _ = tiles.shape
    half = (slots - 1) // 2
    devices = groups * members
    lists = corner_lists(half)
    axes = ("grp", "mem")
    forward = [(index, index + 1) for index in range(devices - 1)]
    backward = [(index + 1, index) for index in range(devices - 1)]

    down_near, up_near, down_far, up_far = pack(tiles, mask, lists)
    above_near = lax.ppermute(down_near, axes, forward)
    below_near = lax.ppermute(up_near, axes, backward)
    above_far = lax.ppermute(down_far, axes, forward)
    below_far = lax.ppermute(up_far, axes, backward)

    square, local_stats, own, cross = local_part(tiles, mask, branch)
    square, near_stats, edge = halo_part(
        own, mask, branch, square, cross, above_near, below_near, lists, False
    )
    updated, far_stats = halo_part(
        own, mask, branch, square, edge, above_far, below_far, lists, True
    )
    order = float(rows * devices * side)
    traces = total_stats((local_stats, near_stats, far_stats), order, groups, members)
    return updated, traces


def solution(mesh):
    placed = (P(("grp", "mem"), None, None, None), P(("grp", "mem"), None), P(("grp", "mem")))
    return jax.shard_map(
        functools.partial(
            on_device, groups=mesh.shape["grp"], members=mesh.shape["mem"]
        ),
        mesh=mesh,
        in_specs=placed,
        out_specs=(P(("grp", "mem"), None, None, None), P()),
        check_vma=False,
    )
```

```python
import functools

import jax
import jax.numpy as jnp
from jax import lax
from jax.experimental import pallas as pl
from jax.experimental.pallas import tpu as pltpu
from jax.sharding import PartitionSpec as P


ANY = pl.BlockSpec(memory_space=pl.ANY)
SMEM = pl.BlockSpec(memory_space=pltpu.SMEM)
VMEM_ALL = pl.BlockSpec(memory_space=pltpu.VMEM)


def nn(left, right):
    return jnp.dot(left, right, preferred_element_type=jnp.float32)


def nt(left, right):
    return lax.dot_general(
        left, right, (((1,), (1,)), ((), ())), preferred_element_type=jnp.float32
    )


def weights(mask, branch):
    keep = mask.astype(jnp.float32)
    return jnp.where(branch == 0, 0.0, 2.0 * keep), jnp.where(branch == 0, keep, -keep)


def finish(square, own, scale):
    return scale[0] * own.astype(jnp.float32) + scale[1] * square


def fold(value):
    return jnp.sum(value.reshape(value.shape[0] // 8, 8, value.shape[1]), axis=0)


def corner_lists(half):
    upper_near = [(c, b) for b in range(1, half) for c in range(b, half)]
    upper_far = [(c, 0) for c in range(half)]
    lower_near = [(c, b) for b in range(half - 1) for c in range(b, half - 1)]
    lower_far = [(half - 1, b) for b in range(half)]
    return upper_near, upper_far, lower_near, lower_far


def triangle(count):
    return count * (count + 1) // 2


def layout(pairs, side):
    off = [pair for pair in pairs if pair[0] != pair[1]]
    diagonal = [pair for pair in pairs if pair[0] == pair[1]]
    first = len(off) * side
    last = first + len(diagonal) * (side // 2)
    spare = -(-len(diagonal) // 16) * 16
    return off, diagonal, first, last, spare


def block_places(small):
    row = lax.broadcasted_iota(jnp.int32, (small, small), 0)
    column = lax.broadcasted_iota(jnp.int32, (small, small), 1)
    return row, column


def pack(tiles, mask, lists):
    rows, slots, side, _ = tiles.shape
    half = (slots - 1) // 2
    small = side // 2
    upper_near, upper_far, lower_near, lower_far = lists
    order = (upper_near, lower_near, upper_far, lower_far)
    plans = [layout(pairs, side) for pairs in order]
    total = sum(len(pairs) for pairs in order)
    diagonals = sum(len(plan[1]) for plan in plans)

    def kernel(tiles_ref, mask_hbm, *refs):
        outs, (held, mask_ref, in_sem, mask_sem) = refs[:4], refs[4:]
        mask_copy = pltpu.make_async_copy(mask_hbm, mask_ref, mask_sem)
        mask_copy.start()
        work = []
        for which, (off, diagonal, first, _, _) in enumerate(plans):
            for index, (c, b) in enumerate(off + diagonal):
                row = rows - half + c if which % 2 == 0 else c
                slot = b - c + half
                if c != b:
                    target = outs[which].at[pl.ds(index * side, side)]
                else:
                    target = held.at[sum(item[4] is not None for item in work)]
                copy = pltpu.make_async_copy(
                    tiles_ref.at[row, slot], target, in_sem.at[len(work)]
                )
                copy.start()
                work.append((copy, row, slot, target, index - len(off) if c == b else None, which))
        mask_copy.wait()
        r, c = block_places(small)
        place = 0
        lines = {}
        for copy, row, slot, target, index, which in work:
            copy.wait()

            @pl.when(mask_ref[row, slot] == 0)
            def _():
                target[...] = jnp.zeros((side, side), tiles.dtype)

            if index is None:
                continue
            first, last, spare = plans[which][2:]
            start = first + index * small
            top = held[place, 0:small, 0:small].astype(jnp.float32)
            bottom = held[place, small:side, small:side].astype(jnp.float32)
            outs[which][start : start + small, 0:small] = jnp.where(r >= c, top, bottom).astype(
                tiles.dtype
            )
            outs[which][start : start + small, small:side] = held[place, 0:small, small:side]
            line = jnp.sum(jnp.where(r == c, bottom, 0.0), axis=0, keepdims=True)
            at = lax.broadcasted_iota(jnp.int32, (spare, small), 0) == index
            before = lines.get(which, jnp.zeros((spare, small), jnp.float32))
            lines[which] = jnp.where(at, line, before)
            place += 1
        for which, value in lines.items():
            last, spare = plans[which][3:]
            value = value.astype(tiles.dtype)
            outs[which][last : last + spare, 0:small] = value
            outs[which][last : last + spare, small:side] = value

    return pl.pallas_call(
        kernel,
        out_shape=tuple(
            pltpu.VMEM((plan[3] + plan[4], side), tiles.dtype) for plan in plans
        ),
        in_specs=[pl.BlockSpec(memory_space=pltpu.HBM)] * 2,
        out_specs=(VMEM_ALL,) * 4,
        scratch_shapes=[
            pltpu.VMEM((diagonals, side, side), tiles.dtype),
            pltpu.SMEM(mask.shape, jnp.int32),
            pltpu.SemaphoreType.DMA((total,)),
            pltpu.SemaphoreType.DMA,
        ],
        compiler_params=pltpu.CompilerParams(vmem_limit_bytes=8 * 2**20),
        cost_estimate=pl.CostEstimate(
            flops=0, transcendentals=0, bytes_accessed=4 * total * side * side
        ),
        name="pack",
    )(in_hbm(tiles), in_hbm(mask))


def local_part(tiles, mask, branch):
    rows, slots, side, _ = tiles.shape
    half = (slots - 1) // 2
    corner = triangle(half)
    small = side // 2

    def kernel(
        tiles_ref, mask_ref, branch_ref, out_ref, stats_ref, own, cross,
        left, right, staged, in_sem, out_sem,
    ):
        def cols(start, count):
            return pl.ds(start * side, count * side)

        def load(row, slot):
            return pltpu.make_async_copy(
                tiles_ref.at[row, slot], own.at[row, :, cols(slot, 1)], in_sem.at[row]
            )

        for row in range(rows):
            for slot in range(slots):
                load(row, slot).start()
        stats_ref[...] = jnp.zeros_like(stats_ref)
        for row in range(rows):
            for slot in range(slots):
                load(row, slot).wait()
            for slot in range(slots):

                @pl.when(mask_ref[row, slot] == 0)
                def _():
                    own[row, :, cols(slot, 1)] = jnp.zeros((side, side), own.dtype)

            if row < half:
                for b in range(row, half):
                    left[cols(row, 1), cols(b, 1)] = own[row, :, cols(b - row, 1)]
            k = row - (rows - half)
            if k >= 0:
                for b in range(k + 1):
                    right[cols(k, 1), cols(b, 1)] = own[row, :, cols(rows + b - row + half, 1)]

        def out_copy(row, column):
            return pltpu.make_async_copy(
                staged.at[row, column], out_ref.at[row, column - row + half], out_sem
            )

        def own_block(row, slot, top, start):
            lanes = pl.ds(pl.multiple_of(slot * side + start, small), small)
            return own[row, top : top + small, lanes]

        @pl.loop(0, rows)
        def _(row):
            for d in range(half + 1):

                @pl.when(row + d < rows)
                def _():
                    other = row + d
                    staged[row, other] = nt(
                        own[row, :, cols(d, slots - d)], own[other, :, cols(0, slots - d)]
                    )
                    scale = weights(mask_ref[row, half + d], branch_ref[row])
                    other_scale = weights(mask_ref[other, half - d], branch_ref[other])
                    purity = jnp.zeros((8, small), jnp.float32)
                    trace = jnp.zeros((8, small), jnp.float32)
                    for top in range(0, side, small):
                        for start in range(0, side, small):
                            down, across = slice(top, top + small), slice(start, start + small)
                            raw = staged[row, other, down, across]
                            if d:
                                value = finish(
                                    raw.T, own_block(other, half - d, start, top), other_scale
                                )
                                staged[other, row, across, down] = value
                                purity = purity + fold(value * value)
                            value = finish(raw, own_block(row, half + d, top, start), scale)
                            staged[row, other, down, across] = value
                            purity = purity + fold(value * value)
                            if d == 0 and top == start:
                                r, c = block_places(small)
                                trace = trace + fold(jnp.where(r == c, value, 0.0))
                    out_copy(row, other).start()
                    if d:
                        out_copy(other, row).start()
                    else:
                        stats_ref[8:16, 0:small] += trace
                    stats_ref[0:8, 0:small] += purity

            for b in range(half):
                @pl.when(row <= b)
                def _():
                    start = pl.multiple_of((half - row) * side, side)
                    cross[triangle(b) + row] = nn(
                        own[row, :, pl.ds(start, (b + 1) * side)],
                        left[cols(0, b + 1), cols(b, 1)],
                    )

                @pl.when(row >= rows - half + b)
                def _():
                    first = rows - half + b
                    start = pl.multiple_of((first - row + half) * side, side)
                    cross[corner + triangle(half - 1 - b) + rows - 1 - row] = nn(
                        own[row, :, pl.ds(start, (half - b) * side)],
                        right[cols(b, half - b), cols(b, 1)],
                    )

        for row in range(rows):
            for column in range(rows):
                if abs(row - column) <= half:
                    out_copy(row, column).wait()

    matmuls = 300
    return pl.pallas_call(
        kernel,
        out_shape=(
            jax.ShapeDtypeStruct(tiles.shape, jnp.float32),
            jax.ShapeDtypeStruct((16, side), jnp.float32),
            pltpu.VMEM((rows, side, slots * side), tiles.dtype),
            pltpu.VMEM((2 * corner, side, side), jnp.float32),
        ),
        in_specs=[pl.BlockSpec(memory_space=pltpu.HBM), SMEM, SMEM],
        out_specs=(ANY, VMEM_ALL, VMEM_ALL, VMEM_ALL),
        scratch_shapes=[
            pltpu.VMEM((half * side, half * side), tiles.dtype),
            pltpu.VMEM((half * side, half * side), tiles.dtype),
            pltpu.VMEM((rows, rows, side, side), jnp.float32),
            pltpu.SemaphoreType.DMA((rows,)),
            pltpu.SemaphoreType.DMA,
        ],
        compiler_params=pltpu.CompilerParams(vmem_limit_bytes=22 * 2**20),
        cost_estimate=pl.CostEstimate(
            flops=2 * matmuls * side**3, transcendentals=0, bytes_accessed=6 * tiles.size
        ),
        name="local_part",
    )(in_hbm(tiles), mask, branch)


def halo_part(own, mask, branch, square, partial, above, below, lists, far):
    rows, side, width = own.shape
    slots = width // side
    half = (slots - 1) // 2
    corner = triangle(half)
    upper_near, upper_far, lower_near, lower_far = lists
    small = side // 2
    chunks = (upper_far, lower_far) if far else (upper_near, lower_near)

    jobs = []
    if far:
        jobs += [(0, 0, b, b, b, None) for b in range(half)]
        jobs += [(rows - 1, 1, b, half + 1 + b, half + b, None) for b in range(half)]
    else:
        for a in range(half):
            for b in range(a, half):
                jobs.append((a, 0, b, b - a, triangle(b) + a, None if a else b))
            row = rows - 1 - a
            for b in range(half - a):
                place = corner + triangle(half - 1 - b) + a
                jobs.append((row, 1, b, rows + b - row + half, place, None if a else half + b))
    finals = sum(job[5] is None for job in jobs)

    def kernel(own_ref, mask_ref, branch_ref, square_ref, partial_ref, above_ref, below_ref, *refs):
        if far:
            out_ref, stats_ref, held, staged, out_sem = refs
        else:
            out_ref, stats_ref, edge_ref, held, staged, out_sem = refs

        def cols(start, count):
            return pl.ds(start * side, count * side)

        r, c = block_places(small)
        for which, (source, pairs) in enumerate(zip((above_ref, below_ref), chunks)):
            off, diagonal, first, last, _ = layout(pairs, side)
            for index, (i, j) in enumerate(off):
                held[which, cols(i, 1), cols(j, 1)] = source[index * side : (index + 1) * side]
            for index, (i, _) in enumerate(diagonal):
                low, mid, high = i * side, i * side + small, (i + 1) * side
                start = first + index * small
                mixed = source[start : start + small, 0:small].astype(jnp.float32)
                flipped = mixed.T
                line = source[last : last + 16, 0:small].astype(jnp.float32)[index : index + 1]
                bottom = jnp.where(r == c, line, jnp.where(r < c, mixed, flipped))
                side_block = source[start : start + small, small:side]
                held[which, low:mid, low:mid] = jnp.where(r >= c, mixed, flipped).astype(own.dtype)
                held[which, low:mid, mid:high] = side_block
                held[which, mid:high, low:mid] = (
                    side_block.astype(jnp.float32).T.astype(own.dtype)
                )
                held[which, mid:high, mid:high] = bottom.astype(own.dtype)

        outs = []
        stats_ref[...] = jnp.zeros_like(stats_ref)
        for row, which, b, slot, place, edge in jobs:
            base = -row if which == 0 else rows - row + half

            def straight(low, high):
                return nn(
                    own_ref[row, :, cols(base + low, high - low)],
                    held[which, cols(low, high - low), cols(b, 1)],
                )

            def turned(low, high):
                return nt(
                    own_ref[row, :, cols(base + low, high - low)],
                    held[which, cols(b, 1), cols(low, high - low)],
                )

            if far and which == 0:
                products = [straight(0, half)] if b == 0 else [turned(0, 1)]
            elif far:
                last = half - 1
                products = [turned(0, half)] if b == last else [straight(last, half)]
            else:
                away = row if which == 0 else rows - 1 - row
                low = max(away, 1) if which == 0 else 0
                high = half if which == 0 else half - max(away, 1)
                products = []
                if low <= b < high:
                    products = [straight(b, high)]
                    if b > low:
                        products.append(turned(low, b))
            value = partial_ref[place]
            for product in products:
                value = value + product
            if edge is not None:
                edge_ref[edge] = value
                continue
            index = len(outs)
            staged[index] = value
            scale = weights(mask_ref[row, slot], branch_ref[row])
            purity = jnp.zeros((8, side), jnp.float32)
            for top in range(0, side, small // 2):
                down = slice(top, top + small // 2)
                value = finish(staged[index, down], own_ref[row, down, cols(slot, 1)], scale)
                staged[index, down] = value
                purity = purity + fold(value * value)
            stats_ref[0:8] += purity
            out = pltpu.make_async_copy(staged.at[index], out_ref.at[row, slot], out_sem.at[index])
            out.start()
            outs.append(out)
        for out in outs:
            out.wait()

    out_shape = [
        jax.ShapeDtypeStruct(square.shape, jnp.float32),
        jax.ShapeDtypeStruct((16, side), jnp.float32),
    ]
    if not far:
        out_shape.append(pltpu.VMEM((2 * half, side, side), jnp.float32))
    return pl.pallas_call(
        kernel,
        out_shape=tuple(out_shape),
        in_specs=[VMEM_ALL, SMEM, SMEM, ANY, VMEM_ALL, VMEM_ALL, VMEM_ALL],
        out_specs=(ANY,) + (VMEM_ALL,) * (len(out_shape) - 1),
        scratch_shapes=[
            pltpu.VMEM((2, half * side, half * side), own.dtype),
            pltpu.VMEM((finals, side, side), jnp.float32),
            pltpu.SemaphoreType.DMA((finals,)),
        ],
        input_output_aliases={3: 0},
        compiler_params=pltpu.CompilerParams(vmem_limit_bytes=(16 if far else 20) * 2**20),
        cost_estimate=pl.CostEstimate(
            flops=2 * (18 if far else 92) * side**3,
            transcendentals=0,
            bytes_accessed=4 * finals * side * side,
        ),
        name="halo_far" if far else "halo_near",
    )(
        in_vmem(own), mask, branch, square, in_vmem(partial), in_vmem(above), in_vmem(below)
    )


def in_hbm(value):
    return pltpu.with_memory_space_constraint(value, pltpu.HBM)


def in_vmem(value):
    return pltpu.with_memory_space_constraint(value, pltpu.VMEM)


def total_stats(stats, order, groups, members):
    devices = groups * members

    def kernel(*refs):
        stat_refs = refs[: len(stats)]
        out_ref, mine, slots, send_sem, recv_sem = refs[len(stats) :]
        me = lax.axis_index("grp") * members + lax.axis_index("mem")
        barrier = pltpu.get_barrier_semaphore()

        def place(step):
            other = lax.rem(me + step, devices)
            return other, (lax.div(other, members), lax.rem(other, members))

        def greet(step, carry):
            pl.semaphore_signal(
                barrier, 1, device_id=place(step)[1], device_id_type=pl.DeviceIdType.MESH
            )
            return carry

        lax.fori_loop(1, devices, greet, 0)
        summed = stat_refs[0][...]
        for ref in stat_refs[1:]:
            summed = summed + ref[...]
        purity = jnp.sum(summed[0:8])
        trace = jnp.sum(summed[8:16])
        lane = lax.broadcasted_iota(jnp.int32, (8, 128), 1)
        mine[...] = jnp.where(lane == 0, trace, purity)
        slots[me] = mine[...]
        pl.semaphore_wait(barrier, devices - 1)

        def copy(step, slot):
            return pltpu.make_async_remote_copy(
                mine, slots.at[slot], send_sem.at[step], recv_sem.at[slot],
                device_id=place(step)[1], device_id_type=pl.DeviceIdType.MESH,
            )

        def begin(step, carry):
            copy(step, me).start()
            return carry

        def end(step, carry):
            copy(step, place(step)[0]).wait_recv()
            return carry

        def leave(step, carry):
            copy(step, me).wait_send()
            return carry

        lax.fori_loop(1, devices, begin, 0)
        lax.fori_loop(1, devices, end, 0)
        whole = slots[0]
        for index in range(1, devices):
            whole = whole + slots[index]
        out_ref[...] = whole / order
        lax.fori_loop(1, devices, leave, 0)

    result = pl.pallas_call(
        kernel,
        out_shape=jax.ShapeDtypeStruct((8, 128), jnp.float32),
        in_specs=[VMEM_ALL] * len(stats),
        out_specs=VMEM_ALL,
        scratch_shapes=[
            pltpu.VMEM((8, 128), jnp.float32),
            pltpu.VMEM((devices, 8, 128), jnp.float32),
            pltpu.SemaphoreType.DMA((devices,)),
            pltpu.SemaphoreType.DMA((devices,)),
        ],
        compiler_params=pltpu.CompilerParams(
            collective_id=0, has_side_effects=True, vmem_limit_bytes=4 * 2**20
        ),
        name="total_stats",
    )(*stats)
    return result[0, 0:2]


def on_device(tiles, mask, branch, groups, members):
    rows, slots, side, _ = tiles.shape
    half = (slots - 1) // 2
    devices = groups * members
    lists = corner_lists(half)
    axes = ("grp", "mem")
    forward = [(index, index + 1) for index in range(devices - 1)]
    backward = [(index + 1, index) for index in range(devices - 1)]

    down_near, up_near, down_far, up_far = pack(tiles, mask, lists)
    above_near = lax.ppermute(down_near, axes, forward)
    below_near = lax.ppermute(up_near, axes, backward)
    above_far = lax.ppermute(down_far, axes, forward)
    below_far = lax.ppermute(up_far, axes, backward)

    square, local_stats, own, cross = local_part(tiles, mask, branch)
    square, near_stats, edge = halo_part(
        own, mask, branch, square, cross, above_near, below_near, lists, False
    )
    updated, far_stats = halo_part(
        own, mask, branch, square, edge, above_far, below_far, lists, True
    )
    order = float(rows * devices * side)
    traces = total_stats((local_stats, near_stats, far_stats), order, groups, members)
    return updated, traces


def solution(mesh):
    placed = (P(("grp", "mem"), None, None, None), P(("grp", "mem"), None), P(("grp", "mem")))
    return jax.shard_map(
        functools.partial(
            on_device, groups=mesh.shape["grp"], members=mesh.shape["mem"]
        ),
        mesh=mesh,
        in_specs=placed,
        out_specs=(P(("grp", "mem"), None, None, None), P()),
        check_vma=False,
    )
```
